512 devices in a mesh: dom: 64 (over z_lo, x, y), snap: 8 (over z_hi, core).
Axes of the slice: x: 4, y: 8, z: 8 (z_hi: 4, z_lo: 2; z = z_hi * 2 + z_lo), core: 2. Of those that a mesh axis runs over, the one named last changes fastest.
Arguments:
- features: bfloat16 [8, 8192, 256], P('snap', 'dom'), may hold values from -6 to 6
- cotangent: bfloat16 [8, 8192, 256], P('snap', 'dom'), may hold values from -6 to 6
- neighbours: int32 [8192, 16], P('dom'), may hold values from 0 to 8191, as said below
- degrees: int32 [8192], P('dom'), may hold values from 1 to 16
- message_proj: bfloat16 [256, 256], replicated, may hold values from -0.375 to 0.375
- combine_proj: bfloat16 [256, 256], replicated, may hold values from -0.375 to 0.375
- attend_proj: bfloat16 [256, 768], replicated, may hold values from -0.375 to 0.375
- output_proj: bfloat16 [256, 256], replicated, may hold values from -0.375 to 0.375
Outputs:
- grad_features: bfloat16 [8, 8192, 256], P('snap', 'dom')
- grad_message: float32 [256, 256], replicated
- grad_combine: float32 [256, 256], replicated
- grad_attend: float32 [256, 768], replicated
- grad_output: float32 [256, 256], replicated
The draws below stay inside these ranges and needn't reach their ends.
Inputs may be any that keep to these rules, and one draw needn't show every extreme that they name: `neighbours`: a neighbour of a node in rows p * 128 to (p + 1) * 128 - 1 lies in rows p * 128 - 128 to (p + 1) * 128 + 127; slot 0 of the first and of the second node of such a block names the lowest and the highest of those rows that exist.
All inputs are finite; a program needn't handle non-finite values.
Results may differ from the reference program's by a relative error of at most 0.012.
Values may be sent and summed in bfloat16 or wider, within the bound.
No kernel may reach another device: no remote copies, remote signals or barrier semaphores. Data moves between devices by JAX's collectives and lax.ppermute only.
A program may use at most 64 MiB of HBM per device.

```python
import math
import jax
import jax.numpy as jnp
from jax import lax

D = 256
HEAD_DIM = 32
SNAPS = 8
DEGREE = 16
NODE_DEV = 128
HALO = 128
NODES = 8192


def draw_neighbours(key, part):
    node_rows = jnp.arange(NODES, dtype=jnp.int32)
    owner_part = node_rows // NODE_DEV
    lowest = jnp.maximum(owner_part * NODE_DEV - HALO, 0)
    highest = jnp.minimum((owner_part + 1) * NODE_DEV + HALO, NODES)
    random_bits = jax.random.randint(key, (NODES, DEGREE), 0, 1 << 30, dtype=jnp.int32)
    picked = lowest[:, None] + random_bits % (highest - lowest)[:, None]
    position = node_rows % NODE_DEV
    slot_index = jnp.arange(DEGREE, dtype=jnp.int32)[None, :]
    picked = jnp.where((position[:, None] == 0) & (slot_index == 0), lowest[:, None], picked)
    picked = jnp.where((position[:, None] == 1) & (slot_index == 0), highest[:, None] - 1, picked)
    return picked.astype(jnp.int32)


def touch_ends(entries, key, least, largest):
    longest = entries.shape.index(max(entries.shape))
    spots = []
    for shift in (0, 1):
        where = [jax.random.randint(jax.random.fold_in(key, axis), (), 0, length) for axis, length in enumerate(entries.shape)]
        where[longest] = (where[longest] + shift) % entries.shape[longest]
        spots.append(tuple(where))
    return entries.at[spots[0]].set(least).at[spots[1]].set(largest)


def levels(own_key, shape, split, low, top_value):
    gain = 1.0
    for dim, blocks in split:
        draws = jax.random.uniform(jax.random.fold_in(jax.random.fold_in(own_key, 6), dim), (blocks,), jnp.float32, low / len(split), top_value / len(split))
        gain = gain * jnp.repeat(jnp.exp(draws), shape[dim] // blocks).reshape((-1,) + (1,) * (len(shape) - 1 - dim))
    return gain


def centred(key, extent, width, most, split=(), held_as=jnp.bfloat16):
    loudness = levels(key, extent, split, -0.22, 0.18) if split else 1.0
    array = jax.random.normal(key, extent, jnp.float32) * width * loudness
    return jnp.minimum(jnp.maximum(array, -most), most).astype(held_as)


def setup_inputs(seed: int = 0) -> dict:
    key_list = jax.random.split(jax.random.key(seed), 9)
    return {
        "features": centred(key_list[0], (SNAPS, NODES, D), 1.0, 6.0, ((0, 8), (1, 64))),
        "cotangent": centred(key_list[1], (SNAPS, NODES, D), 1.0, 6.0, ((0, 8), (1, 64))),
        "neighbours": draw_neighbours(jax.random.fold_in(key_list[8], 71), 0),
        "degrees": touch_ends(jax.random.randint(key_list[3], (NODES,), 1, DEGREE + 1), jax.random.fold_in(key_list[3], 1), 1, DEGREE).astype(jnp.int32),
        "message_proj": centred(key_list[4], (D, D), D ** -0.5, 0.375),
        "combine_proj": centred(key_list[5], (D, D), D ** -0.5, 0.375),
        "attend_proj": centred(key_list[6], (D, 3 * D), D ** -0.5, 0.375),
        "output_proj": centred(key_list[7], (D, D), D ** -0.5, 0.375),
    }


def silu_slope(inputs_pre):
    logistic = jax.nn.sigmoid(inputs_pre)
    return logistic * (1.0 + inputs_pre * (1.0 - logistic))

def edge_inputs(message_rows, own_block, neighbour_block, degree_block):
    gathered = jnp.take(message_rows, neighbour_block, axis=0)
    before = gathered + own_block.astype(jnp.float32)[:, None, :]
    slot_index = jnp.arange(neighbour_block.shape[1], dtype=jnp.int32)
    used = (slot_index[None, :] < degree_block[:, None]).astype(jnp.float32)
    weights = used / degree_block.astype(jnp.float32)[:, None]
    return (before, weights)

def spatial_forward(own_rows, message_rows, neighbour_index, degrees, combine_proj, block_rows):
    node_count = own_rows.shape[0]

    def per_block(block_index):
        offset = block_index * block_rows
        own_block = lax.dynamic_slice_in_dim(own_rows, offset, block_rows, 0)
        neighbour_block = lax.dynamic_slice_in_dim(neighbour_index, offset, block_rows, 0)
        degree_block = lax.dynamic_slice_in_dim(degrees, offset, block_rows, 0)
        before, weights = edge_inputs(message_rows, own_block, neighbour_block, degree_block)
        return lax.optimization_barrier(jnp.sum(jax.nn.silu(before) * weights[:, :, None], axis=1))
    combined = lax.map(per_block, jnp.arange(node_count // block_rows, dtype=jnp.int32))
    combined = combined.reshape(node_count, -1).astype(jnp.bfloat16)
    spatial = own_rows.astype(jnp.float32) + jnp.dot(combined, combine_proj, preferred_element_type=jnp.float32)
    return (combined, spatial.astype(jnp.bfloat16))

def spatial_backward(own_rows, message_rows, neighbour_index, degrees, grad_spatial, combine_proj, block_rows):
    node_count = own_rows.shape[0]
    feature_width = own_rows.shape[1]
    grad_combined = jnp.dot(grad_spatial, combine_proj.T, preferred_element_type=jnp.float32)

    def per_block(totals, block_index):
        offset = block_index * block_rows
        own_block = lax.dynamic_slice_in_dim(own_rows, offset, block_rows, 0)
        neighbour_block = lax.dynamic_slice_in_dim(neighbour_index, offset, block_rows, 0)
        degree_block = lax.dynamic_slice_in_dim(degrees, offset, block_rows, 0)
        grad_block = lax.dynamic_slice_in_dim(grad_combined, offset, block_rows, 0)
        before, weights = edge_inputs(message_rows, own_block, neighbour_block, degree_block)
        grad_before = grad_block[:, None, :] * weights[:, :, None] * silu_slope(before)
        totals = totals.at[neighbour_block.reshape(-1)].add(grad_before.reshape(-1, feature_width))
        return (totals, lax.optimization_barrier(jnp.sum(grad_before, axis=1)))
    start_rows = jnp.zeros((message_rows.shape[0], feature_width), jnp.float32)
    grad_rows, self_terms = lax.scan(per_block, start_rows, jnp.arange(node_count // block_rows, dtype=jnp.int32))
    return (grad_rows, self_terms.reshape(node_count, feature_width))

def temporal_block(spat_block, cot_block, attend_proj, output_proj):
    snap_count, node_count, feature_width = spat_block.shape
    head_count = feature_width // HEAD_DIM
    row_count = snap_count * node_count
    flat_spat = spat_block.reshape(row_count, feature_width)
    flat_cot = cot_block.reshape(row_count, feature_width)
    projected = jnp.dot(flat_spat, attend_proj, preferred_element_type=jnp.float32)
    projected = projected.reshape(snap_count, node_count, 3, head_count, HEAD_DIM)
    query_rows = projected[:, :, 0]
    key_rows = projected[:, :, 1]
    value_rows = projected[:, :, 2]
    inverse_root = 1.0 / math.sqrt(HEAD_DIM)
    precise = lax.Precision.HIGHEST
    scores = jnp.einsum('snhe,rnhe->nhsr', query_rows, key_rows, precision=precise) * inverse_root
    exponent = jnp.exp(scores)
    soft_weights = exponent / lax.optimization_barrier(jnp.sum(exponent, axis=-1, keepdims=True))
    attended = jnp.einsum('nhsr,rnhe->snhe', soft_weights, value_rows, precision=precise)
    attended = attended.reshape(row_count, feature_width).astype(jnp.bfloat16)
    grad_output = jnp.dot(attended.T, flat_cot, preferred_element_type=jnp.float32)
    grad_attended = jnp.dot(flat_cot, output_proj.T, preferred_element_type=jnp.float32)
    grad_attended = grad_attended.reshape(snap_count, node_count, head_count, HEAD_DIM)
    grad_soft = jnp.einsum('snhe,rnhe->nhsr', grad_attended, value_rows, precision=precise)
    grad_value = jnp.einsum('nhsr,snhe->rnhe', soft_weights, grad_attended, precision=precise)
    grad_score = soft_weights * (grad_soft - lax.optimization_barrier(jnp.sum(soft_weights * grad_soft, axis=-1, keepdims=True))) * inverse_root
    grad_query = jnp.einsum('nhsr,rnhe->snhe', grad_score, key_rows, precision=precise)
    grad_key = jnp.einsum('nhsr,snhe->rnhe', grad_score, query_rows, precision=precise)
    grad_three = jnp.stack([grad_query, grad_key, grad_value], axis=2)
    grad_three = grad_three.reshape(row_count, 3 * feature_width).astype(jnp.bfloat16)
    grad_attend = jnp.dot(flat_spat.T, grad_three, preferred_element_type=jnp.float32)
    grad_spatial = flat_cot.astype(jnp.float32) + jnp.dot(grad_three, attend_proj.T, preferred_element_type=jnp.float32)
    grad_spatial = grad_spatial.astype(jnp.bfloat16).reshape(snap_count, node_count, feature_width)
    return (grad_spatial, grad_attend, grad_output)

def reference(features, cotangent, neighbours, degrees, message_proj, combine_proj, attend_proj, output_proj):
    block_rows = NODE_DEV
    message_list = []
    combined_list = []
    spatial_list = []
    for snapshot in range(SNAPS):
        message_rows = jnp.dot(features[snapshot], message_proj, preferred_element_type=jnp.float32)
        combined, spatial = spatial_forward(features[snapshot], message_rows, neighbours, degrees, combine_proj, block_rows)
        message_list.append(message_rows)
        combined_list.append(combined)
        spatial_list.append(spatial)
    spatial_all = jnp.stack(spatial_list)

    def temporal_step(totals, block_index):
        offset = block_index * NODE_DEV
        spat_block = lax.dynamic_slice_in_dim(spatial_all, offset, NODE_DEV, 1)
        cot_block = lax.dynamic_slice_in_dim(cotangent, offset, NODE_DEV, 1)
        grad_block, grad_attend, grad_output = temporal_block(spat_block, cot_block, attend_proj, output_proj)
        buffer = lax.dynamic_update_slice_in_dim(totals[2], grad_block, offset, 1)
        return ((totals[0] + grad_attend, totals[1] + grad_output, buffer), None)
    start_totals = (jnp.zeros((D, 3 * D), jnp.float32), jnp.zeros((D, D), jnp.float32), jnp.zeros((SNAPS, NODES, D), jnp.bfloat16))
    totals, unused_out = lax.scan(temporal_step, start_totals, jnp.arange(NODES // NODE_DEV, dtype=jnp.int32))
    raw_attend, raw_output, grad_spatial_all = totals
    raw_message = jnp.zeros((D, D), jnp.float32)
    raw_combine = jnp.zeros((D, D), jnp.float32)
    grad_list = []
    for snapshot in range(SNAPS):
        grad_spatial = grad_spatial_all[snapshot]
        raw_combine = raw_combine + jnp.dot(combined_list[snapshot].T, grad_spatial, preferred_element_type=jnp.float32)
        grad_rows, self_terms = spatial_backward(features[snapshot], message_list[snapshot], neighbours, degrees, grad_spatial, combine_proj, block_rows)
        grad_rows = grad_rows.astype(jnp.bfloat16)
        raw_message = raw_message + jnp.dot(features[snapshot].T, grad_rows, preferred_element_type=jnp.float32)
        grad_here = grad_spatial.astype(jnp.float32) + self_terms
        grad_here = grad_here + jnp.dot(grad_rows, message_proj.T, preferred_element_type=jnp.float32)
        grad_list.append(grad_here.astype(jnp.bfloat16))
    factor = 1.0 / math.sqrt(SNAPS * NODES)
    grad_features = jnp.stack(grad_list)
    return (grad_features, raw_message * factor, raw_combine * factor, raw_attend * factor, raw_output * factor)
```

```python
import math

import jax
import jax.numpy as jnp
import numpy as np
from jax import lax
from jax.experimental import pallas as pl
from jax.experimental.pallas import tpu as pltpu
from jax.sharding import Mesh
from jax.sharding import PartitionSpec as P

HEAD_DIM = 32
SNAPS = 8
HALO = 128
WIDTH = 256
SLOTS = 16
LANES = 128

FINE = (2, 4, 8, 4, 2)
FINE_NAMES = ("zl", "x", "y", "zh", "c")
DOM = ("zl", "x", "y")
SNAP = ("zh", "c")
SCATTER = ("zl", "y")
ACROSS = ("x", "zh")

f32 = jnp.float32
bf16 = jnp.bfloat16
VMEM = pl.BlockSpec(memory_space=pltpu.VMEM)


def call(kernel, outs, args, scratch=(), name=None):
    return pl.pallas_call(
        kernel,
        out_shape=[jax.ShapeDtypeStruct(s, d) for s, d in outs],
        in_specs=[VMEM] * len(args),
        out_specs=[VMEM] * len(outs),
        scratch_shapes=list(scratch),
        name=name,
    )(*args)


def mm(a, b):
    return jnp.dot(a, b, preferred_element_type=f32)


def mm_nt(a, b):
    return lax.dot_general(a, b, (((1,), (1,)), ((), ())), preferred_element_type=f32)


def mm_tn(a, b):
    return lax.dot_general(a, b, (((0,), (0,)), ((), ())), preferred_element_type=f32)


def put_slab(ref, index, value):
    base = index * 2 * WIDTH
    value = value.astype(ref.dtype)
    ref[base : base + WIDTH, :] = value[:, :LANES]
    ref[base + WIDTH : base + 2 * WIDTH, :] = value[:, LANES:]


def forward_kernel(left, own, right, nbr, deg, mproj, cproj, combined, spatial, slopew, ext, hot):
    ext[:HALO] = left[...]
    ext[HALO : HALO + 128] = own[...]
    ext[HALO + 128 :] = right[...]
    rows = own.shape[0]
    own_f = own[...].astype(f32)
    lanes = lax.broadcasted_iota(jnp.int32, (rows, 3 * HALO), 1)
    for k in range(SLOTS):
        mark = nbr[:, k : k + 1] == lanes
        hot[k * rows : (k + 1) * rows] = jnp.where(mark, 1.0, 0.0).astype(bf16)
    degree = deg[...]
    share = 1.0 / degree.astype(f32)
    total = jnp.zeros((rows, WIDTH), f32)
    group = 4
    for g in range(SLOTS // group):
        span = group * rows
        picked = mm(hot[g * span : (g + 1) * span], ext[...]).astype(bf16)
        message = mm(picked, mproj[...])
        for j in range(group):
            k = g * group + j
            weight = jnp.where(degree > k, share, 0.0)
            before = message[j * rows : (j + 1) * rows] + own_f
            logistic = 0.5 * jnp.tanh(0.5 * before) + 0.5
            value = before * logistic
            total = total + value * weight
            slope = logistic + logistic * (before - value)
            slopew[k * rows : (k + 1) * rows] = (slope * weight).astype(bf16)
    comb = total.astype(bf16)
    combined[...] = comb
    spatial[...] = (own_f + mm(comb, cproj[...])).astype(bf16)


def temporal_kernel(spat, cot, aproj, oproj, grad_spatial, attend_out, output_out, prods, sums):
    snaps, nodes, _ = spat.shape
    rows = snaps * nodes
    x = spat[...].reshape(rows, WIDTH)
    c = cot[...].reshape(rows, WIDTH)
    projected = mm(x, aproj[...])
    inverse_root = 1.0 / math.sqrt(HEAD_DIM)
    qs = projected[:, :WIDTH] * inverse_root
    key = projected[:, WIDTH : 2 * WIDTH]
    val = projected[:, 2 * WIDTH :]
    da = mm_nt(c, oproj[...])

    def split(at, value):
        high = value.astype(bf16)
        prods[at : at + rows, :WIDTH] = high
        prods[at : at + rows, WIDTH:] = (value - high.astype(f32)).astype(bf16)

    key3 = key.reshape(snaps, nodes, WIDTH)
    val3 = val.reshape(snaps, nodes, WIDTH)
    for s in range(snaps):
        one = slice(s * nodes, (s + 1) * nodes)
        split(s * rows, (qs[one][None] * key3).reshape(rows, WIDTH))
        split((snaps + s) * rows, (da[one][None] * val3).reshape(rows, WIDTH))
    i = lax.broadcasted_iota(jnp.int32, (2 * WIDTH, WIDTH), 0)
    j = lax.broadcasted_iota(jnp.int32, (2 * WIDTH, WIDTH), 1)
    same = (i & (WIDTH - 1)) // HEAD_DIM == j // HEAD_DIM
    same = jnp.where(same, 1.0, 0.0).astype(bf16)
    step = 4 * rows
    for at in range(0, 2 * snaps * rows, step):
        sums[at : at + step] = mm(prods[at : at + step], same)

    grad_key = jnp.zeros((snaps, nodes, WIDTH), f32)
    grad_val = jnp.zeros((snaps, nodes, WIDTH), f32)
    attended = []
    grad_query = []
    for s in range(snaps):
        one = slice(s * nodes, (s + 1) * nodes)
        exponent = jnp.exp(sums[s * rows : (s + 1) * rows]).reshape(snaps, nodes, WIDTH)
        soft = exponent * (1.0 / jnp.sum(exponent, axis=0))[None]
        attended.append(jnp.sum(soft * val3, axis=0))
        grad_soft = sums[(snaps + s) * rows : (snaps + s + 1) * rows].reshape(snaps, nodes, WIDTH)
        mean = jnp.sum(soft * grad_soft, axis=0)
        grad_score = soft * (grad_soft - mean[None])
        grad_query.append(jnp.sum(grad_score * key3, axis=0) * inverse_root)
        grad_key = grad_key + grad_score * qs[one][None]
        grad_val = grad_val + soft * da[one][None]
    att = jnp.concatenate(attended, axis=0).astype(bf16)
    put_slab(output_out, 0, mm_tn(att, c))
    parts = (
        jnp.concatenate(grad_query, axis=0).astype(bf16),
        grad_key.reshape(rows, WIDTH).astype(bf16),
        grad_val.reshape(rows, WIDTH).astype(bf16),
    )
    total = c.astype(f32)
    for p, part in enumerate(parts):
        put_slab(attend_out, p, mm_tn(x, part))
        total = total + mm_nt(part, aproj[:, p * WIDTH : (p + 1) * WIDTH])
    grad_spatial[...] = total.astype(bf16).reshape(snaps, nodes, WIDTH)


def backward_kernel(
    gs_ref, comb, slopew, nbrt, left, own, right, cproj, att_in, out_in,
    ghosts, own_rows, base, partial, hot, gb
):
    rows = own.shape[0]
    gs = gs_ref[...]
    gc = mm_nt(gs, cproj[...])
    below = lax.broadcasted_iota(jnp.int32, (3 * HALO, rows), 0)
    total = gs.astype(f32)
    for k in range(SLOTS):
        span = slice(k * rows, (k + 1) * rows)
        hot[:, span] = jnp.where(nbrt[k : k + 1, :] == below, 1.0, 0.0).astype(bf16)
        grad_before = gc * slopew[span].astype(f32)
        total = total + grad_before
        gb[span] = grad_before.astype(bf16)
    base[...] = total
    grad_rows = mm(hot[...], gb[...])
    ghosts[0] = grad_rows[:HALO].astype(bf16)
    ghosts[1] = grad_rows[HALO + rows :].astype(bf16)
    own_rows[...] = grad_rows[HALO : HALO + rows]
    rounded = grad_rows.astype(bf16)
    message = mm_tn(left[...], rounded[:HALO])
    message = message + mm_tn(own[...], rounded[HALO : HALO + rows])
    message = message + mm_tn(right[...], rounded[HALO + rows :])
    partial[0] = att_in[...]
    partial[1, : 2 * WIDTH] = out_in[...]
    second = partial.at[1]
    put_slab(second, 1, message)
    put_slab(second, 2, mm_tn(comb[...], gs))


def features_kernel(base, own_rows, from_left, from_right, mproj, grad):
    own = own_rows[...] + from_left[...].astype(f32) + from_right[...].astype(f32)
    grad[...] = (base[...] + mm_nt(own.astype(bf16), mproj[...])).astype(bf16)


def pair_kernel(both, out):
    out[...] = (both[0].astype(f32) + both[1].astype(f32)).astype(bf16).reshape(out.shape)


def fold_kernel(parts, out):
    total = parts[0].astype(f32)
    for p in range(1, parts.shape[0]):
        total = total + parts[p].astype(f32)
    total = total.astype(bf16)
    for p in range(out.shape[0]):
        out[p] = total


def final_kernel(factor, sums, message, combine, attend, output):
    def get(half, index):
        base = index * 2 * WIDTH
        first = sums[half, base : base + WIDTH, :].astype(f32) * factor
        second = sums[half, base + WIDTH : base + 2 * WIDTH, :].astype(f32) * factor
        return first, second

    def put(ref, at, pair):
        ref[:, at : at + LANES] = pair[0]
        ref[:, at + LANES : at + 2 * LANES] = pair[1]

    for p in range(3):
        put(attend, p * WIDTH, get(0, p))
    put(output, 0, get(1, 0))
    put(message, 0, get(1, 1))
    put(combine, 0, get(1, 2))


def swap(x, axes):
    return lax.all_to_all(x, axes, split_axis=0, concat_axis=0, tiled=True)


def body(features, cotangent, neighbours, degrees, mproj, cproj, aproj, oproj):
    _, rows, width = features.shape
    dom_size = lax.axis_size(DOM)
    up = [(i, i + 1) for i in range(dom_size - 1)]
    down = [(i + 1, i) for i in range(dom_size - 1)]
    own = features[0]
    from_left = lax.ppermute(own, DOM, up)
    from_right = lax.ppermute(own, DOM, down)
    first_row = lax.axis_index(DOM) * rows - HALO
    nbr = neighbours - first_row
    nbrt = nbr.T
    deg = degrees.reshape(rows, 1)
    edges = SLOTS * rows
    combined, spatial, slopew = call(
        forward_kernel,
        [((rows, width), bf16), ((rows, width), bf16), ((edges, width), bf16)],
        (from_left, own, from_right, nbr, deg, mproj, cproj),
        [pltpu.VMEM((3 * HALO, width), bf16), pltpu.VMEM((edges, 3 * HALO), bf16)],
        "forward",
    )
    share = rows // SNAPS
    sent = jnp.stack([spatial.reshape(SNAPS, share, width), cotangent[0].reshape(SNAPS, share, width)], axis=1)
    got = swap(sent, SNAP)
    grads, attend_part, output_part = call(
        temporal_kernel,
        [((SNAPS, share, width), bf16), ((6 * width, LANES), bf16), ((2 * width, LANES), bf16)],
        (got[:, 0], got[:, 1], aproj, oproj),
        [pltpu.VMEM((2 * SNAPS * rows, 2 * width), bf16), pltpu.VMEM((2 * SNAPS * rows, width), f32)],
        "temporal",
    )
    grad_spatial = swap(grads, SNAP).reshape(rows, width)
    ghosts, own_rows, base, partial = call(
        backward_kernel,
        [((2, HALO, width), bf16), ((rows, width), f32), ((rows, width), f32), ((2, 6 * width, LANES), bf16)],
        (grad_spatial, combined, slopew, nbrt, from_left, own, from_right, cproj, attend_part, output_part),
        [pltpu.VMEM((3 * HALO, edges), bf16), pltpu.VMEM((edges, width), bf16)],
        "backward",
    )
    back_left = lax.ppermute(ghosts[1], DOM, up)
    back_right = lax.ppermute(ghosts[0], DOM, down)
    (grad_features,) = call(
        features_kernel,
        [((rows, width), bf16)],
        (base, own_rows, back_left, back_right, mproj),
        name="features",
    )
    both = swap(partial, "c")
    count = lax.axis_size(SCATTER)
    across = lax.axis_size(ACROSS)
    piece = 6 * width // count
    (mine,) = call(pair_kernel, [((count, piece, LANES), bf16)], (both,), name="pair")
    (spread,) = call(fold_kernel, [((across, piece, LANES), bf16)], (swap(mine, SCATTER),), name="fold")
    (whole,) = call(fold_kernel, [((count, piece, LANES), bf16)], (swap(spread, ACROSS),), name="fold_all")
    half = swap(whole, SCATTER).reshape(6 * width, LANES)
    sums = lax.all_gather(half, "c", axis=0)
    factor = 1.0 / math.sqrt(SNAPS * dom_size * rows)

    def last(*refs):
        final_kernel(factor, *refs)

    message, combine, attend, output = call(
        last,
        [((width, width), f32), ((width, width), f32), ((width, 3 * width), f32), ((width, width), f32)],
        (sums,),
        name="final",
    )
    return grad_features[None], message, combine, attend, output


def build(mesh, fine):
    fine_mesh = Mesh(np.asarray(mesh.devices).reshape(fine), FINE_NAMES)
    in_specs = (
        P(SNAP, DOM, None),
        P(SNAP, DOM, None),
        P(DOM, None),
        P(DOM),
        P(),
        P(),
        P(),
        P(),
    )
    out_specs = (P(SNAP, DOM, None), P(), P(), P(), P())
    return jax.shard_map(body, mesh=fine_mesh, in_specs=in_specs, out_specs=out_specs, check_vma=False)


def solution(mesh):
    return build(mesh, FINE)
```

```python
import math

import jax
import jax.numpy as jnp
import numpy as np
from jax import lax
from jax.experimental import pallas as pl
from jax.experimental.pallas import tpu as pltpu
from jax.sharding import Mesh
from jax.sharding import PartitionSpec as P


HEAD_DIM = 32
SNAPS = 8
HALO = 128
WIDTH = 256
SLOTS = 16
LANES = 128

FINE = (2, 4, 8, 4, 2)
FINE_NAMES = ("zl", "x", "y", "zh", "c")
DOM = ("zl", "x", "y")
SNAP = ("zh", "c")
SCATTER = ("zl", "y")
ACROSS = ("x", "zh")

f32 = jnp.float32
bf16 = jnp.bfloat16
VMEM = pl.BlockSpec(memory_space=pltpu.VMEM)
SMEM = pl.BlockSpec(memory_space=pltpu.SMEM)


def call(kernel, outs, args, scratch=(), scalars=0, stored=False):
    bound = []
    for n, a in enumerate(args):
        bound.append(a if n < scalars else pltpu.with_memory_space_constraint(a, pltpu.VMEM))
    place = jax.ShapeDtypeStruct if stored else pltpu.VMEM
    return pl.pallas_call(
        kernel,
        out_shape=[place(s, d) for s, d in outs],
        in_specs=[SMEM if n < scalars else VMEM for n in range(len(args))],
        out_specs=[VMEM] * len(outs),
        scratch_shapes=list(scratch),
        compiler_params=pltpu.CompilerParams(vmem_limit_bytes=24 * 2**20),
    )(*bound)


def mm(a, b):
    return jnp.dot(a, b, preferred_element_type=f32)


def mm_nt(a, b):
    return lax.dot_general(a, b, (((1,), (1,)), ((), ())), preferred_element_type=f32)


def mm_tn(a, b):
    return lax.dot_general(a, b, (((0,), (0,)), ((), ())), preferred_element_type=f32)


def put_slab(ref, index, value):
    base = index * 2 * WIDTH
    value = value.astype(ref.dtype)
    ref[base : base + WIDTH, :] = value[:, :LANES]
    ref[base + WIDTH : base + 2 * WIDTH, :] = value[:, LANES:]


def slots_kernel(
    first_row, nbr_in, deg_in, own, cot, mproj, cproj,
    hot, weights, nbrt, own_out, cot_out, mproj_out, cproj_out, table_in, deg, sems
):
    moves = ((nbr_in, table_in), (deg_in, deg), (own, own_out), (cot, cot_out), (mproj, mproj_out), (cproj, cproj_out))
    copies = [pltpu.make_async_copy(a, b, sems.at[n]) for n, (a, b) in enumerate(moves)]
    for copy in copies:
        copy.start()
    copies[0].wait()
    copies[1].wait()
    slots, rows = nbrt.shape
    local = table_in[...] - first_row[0]
    nbrt[...] = local
    pad = jnp.zeros((rows - slots - 1, rows), f32)
    table = jnp.concatenate([local.astype(f32), deg[...].astype(f32), pad], axis=0).T
    lanes = lax.broadcasted_iota(jnp.int32, (rows, 3 * HALO), 1).astype(f32)
    for k in range(slots):
        mark = table[:, k : k + 1] == lanes
        hot[k * rows : (k + 1) * rows] = jnp.where(mark, 1.0, 0.0).astype(bf16)
    degree = table[:, slots : slots + 1]
    slot = lax.broadcasted_iota(jnp.int32, (rows, slots), 1).astype(f32)
    weights[...] = jnp.where(slot < degree, 1.0 / degree, 0.0)
    for copy in copies[2:]:
        copy.wait()


def forward_kernel(left, own, right, cot, hot, weights, mproj, cproj, combined, sent, slopew, ext):
    ext[:HALO] = left[...]
    ext[HALO : HALO + 128] = own[...]
    ext[HALO + 128 :] = right[...]
    rows = own.shape[0]
    own_f = own[...].astype(f32)
    total = jnp.zeros((rows, WIDTH), f32)
    group = 4
    for g in range(SLOTS // group):
        span = group * rows
        picked = mm(hot[g * span : (g + 1) * span], ext[...]).astype(bf16)
        message = mm(picked, mproj[...])
        for j in range(group):
            k = g * group + j
            weight = weights[:, k : k + 1]
            before = message[j * rows : (j + 1) * rows] + own_f
            logistic = 0.5 * jnp.tanh(0.5 * before) + 0.5
            value = before * logistic
            total = total + value * weight
            slope = logistic + logistic * (before - value)
            slopew[k * rows : (k + 1) * rows] = (slope * weight).astype(bf16)
    comb = total.astype(bf16)
    combined[...] = comb
    spatial = (own_f + mm(comb, cproj[...])).astype(bf16)
    share = sent.shape[2]
    for s in range(sent.shape[0]):
        sent[s, 0] = spatial[s * share : (s + 1) * share]
        sent[s, 1] = cot[s * share : (s + 1) * share]


def temporal_kernel(got, aproj, oproj, grad_spatial, attend_out, output_out, prods, sums):
    snaps, _, nodes, _ = got.shape
    rows = snaps * nodes
    x = got[:, 0].reshape(rows, WIDTH)
    c = got[:, 1].reshape(rows, WIDTH)
    projected = mm(x, aproj[...])
    inverse_root = 1.0 / math.sqrt(HEAD_DIM)
    qs = projected[:, :WIDTH] * inverse_root
    key = projected[:, WIDTH : 2 * WIDTH]
    val = projected[:, 2 * WIDTH :]
    da = mm_nt(c, oproj[...])

    def split(at, value):
        high = value.astype(bf16)
        prods[at : at + rows, :WIDTH] = high
        prods[at : at + rows, WIDTH:] = (value - high.astype(f32)).astype(bf16)

    key3 = key.reshape(snaps, nodes, WIDTH)
    val3 = val.reshape(snaps, nodes, WIDTH)
    for s in range(snaps):
        one = slice(s * nodes, (s + 1) * nodes)
        split(s * rows, (qs[one][None] * key3).reshape(rows, WIDTH))
        split((snaps + s) * rows, (da[one][None] * val3).reshape(rows, WIDTH))
    i = lax.broadcasted_iota(jnp.int32, (2 * WIDTH, WIDTH), 0)
    j = lax.broadcasted_iota(jnp.int32, (2 * WIDTH, WIDTH), 1)
    same = (i & (WIDTH - 1)) // HEAD_DIM == j // HEAD_DIM
    same = jnp.where(same, 1.0, 0.0).astype(bf16)
    step = 4 * rows
    for at in range(0, 2 * snaps * rows, step):
        sums[at : at + step] = mm(prods[at : at + step], same)

    grad_key = jnp.zeros((snaps, nodes, WIDTH), f32)
    grad_val = jnp.zeros((snaps, nodes, WIDTH), f32)
    attended = []
    grad_query = []
    for s in range(snaps):
        one = slice(s * nodes, (s + 1) * nodes)
        exponent = jnp.exp(sums[s * rows : (s + 1) * rows]).reshape(snaps, nodes, WIDTH)
        soft = exponent * (1.0 / jnp.sum(exponent, axis=0))[None]
        attended.append(jnp.sum(soft * val3, axis=0))
        grad_soft = sums[(snaps + s) * rows : (snaps + s + 1) * rows].reshape(snaps, nodes, WIDTH)
        mean = jnp.sum(soft * grad_soft, axis=0)
        grad_score = soft * (grad_soft - mean[None])
        grad_query.append(jnp.sum(grad_score * key3, axis=0) * inverse_root)
        grad_key = grad_key + grad_score * qs[one][None]
        grad_val = grad_val + soft * da[one][None]
    att = jnp.concatenate(attended, axis=0).astype(bf16)
    put_slab(output_out, 0, mm_tn(att, c))
    parts = (
        jnp.concatenate(grad_query, axis=0).astype(bf16),
        grad_key.reshape(rows, WIDTH).astype(bf16),
        grad_val.reshape(rows, WIDTH).astype(bf16),
    )
    total = c.astype(f32)
    for p, part in enumerate(parts):
        put_slab(attend_out, p, mm_tn(x, part))
        total = total + mm_nt(part, aproj[:, p * WIDTH : (p + 1) * WIDTH])
    grad_spatial[...] = total.astype(bf16).reshape(snaps, nodes, WIDTH)


def backward_kernel(
    core, gs_ref, comb, slopew, nbrt, left, own, right, cproj, att_in, out_in,
    to_left, to_right, own_rows, base, keep, send, gb, other, hot
):
    rows = own.shape[0]
    gs = gs_ref[...]
    gc = mm_nt(gs, cproj[...])
    total = gs.astype(f32)
    below = lax.broadcasted_iota(jnp.int32, (3 * HALO, rows), 0)
    for k in range(SLOTS):
        span = slice(k * rows, (k + 1) * rows)
        hot[:, span] = jnp.where(nbrt[k : k + 1, :] == below, 1.0, 0.0).astype(bf16)
        grad_before = gc * slopew[span].astype(f32)
        total = total + grad_before
        gb[span] = grad_before.astype(bf16)
    base[...] = total
    grad_rows = mm(hot[...], gb[...])
    rounded = grad_rows.astype(bf16)
    to_left[...] = rounded[:HALO]
    to_right[...] = rounded[HALO + rows :]
    own_rows[...] = grad_rows[HALO : HALO + rows]
    message = mm_tn(left[...], rounded[:HALO])
    message = message + mm_tn(own[...], rounded[HALO : HALO + rows])
    message = message + mm_tn(right[...], rounded[HALO + rows :])
    other[: 2 * WIDTH] = out_in[...]
    put_slab(other, 1, message)
    put_slab(other, 2, mm_tn(comb[...], gs))
    first = core[0] == 0
    keep[...] = jnp.where(first, att_in[...], other[...])
    send[0] = jnp.where(first, other[...], att_in[...])


def features_kernel(base, own_rows, from_left, from_right, mproj, grad):
    own = own_rows[...] + from_left[...].astype(f32) + from_right[...].astype(f32)
    grad[...] = (base[...] + mm_nt(own.astype(bf16), mproj[...])).astype(bf16)


def pair_kernel(core, keep, both, out):
    other = jnp.where(core[0] == 0, both[1], both[0])
    out[...] = (keep[...].astype(f32) + other.astype(f32)).astype(bf16).reshape(out.shape)


def fold_kernel(parts, out):
    total = parts[0].astype(f32)
    for p in range(1, parts.shape[0]):
        total = total + parts[p].astype(f32)
    total = total.astype(bf16)
    for p in range(out.shape[0]):
        out[p] = total


def final_kernel(factor, sums, message, combine, attend, output):
    def get(half, index):
        base = index * 2 * WIDTH
        first = sums[half, base : base + WIDTH, :].astype(f32) * factor
        second = sums[half, base + WIDTH : base + 2 * WIDTH, :].astype(f32) * factor
        return first, second

    def put(ref, at, pair):
        ref[:, at : at + LANES] = pair[0]
        ref[:, at + LANES : at + 2 * LANES] = pair[1]

    for p in range(3):
        put(attend, p * WIDTH, get(0, p))
    put(output, 0, get(1, 0))
    put(message, 0, get(1, 1))
    put(combine, 0, get(1, 2))


def swap(x, axes):
    return lax.all_to_all(x, axes, split_axis=0, concat_axis=0, tiled=True)


def step(features, cotangent, neighbours, degrees, mproj, cproj, aproj, oproj):
    _, rows, width = features.shape
    dom_size = lax.axis_size(DOM)
    up = [(i, i + 1) for i in range(dom_size - 1)]
    down = [(i + 1, i) for i in range(dom_size - 1)]
    own = features[0]
    cot = cotangent[0]
    from_left = lax.ppermute(own, DOM, up)
    from_right = lax.ppermute(own, DOM, down)
    first_row = (lax.axis_index(DOM) * rows - HALO).reshape(1)
    core = lax.axis_index("c").reshape(1)
    edges = SLOTS * rows
    stored = [
        pltpu.with_memory_space_constraint(a, pltpu.HBM)
        for a in (neighbours.T, degrees.reshape(1, rows), own, cot, mproj, cproj)
    ]
    hot, weights, nbrt, own, cot, mproj, cproj = pl.pallas_call(
        slots_kernel,
        out_shape=[
            pltpu.VMEM((edges, 3 * HALO), bf16),
            pltpu.VMEM((rows, SLOTS), f32),
            pltpu.VMEM((SLOTS, rows), jnp.int32),
            pltpu.VMEM((rows, width), bf16),
            pltpu.VMEM((rows, width), bf16),
            pltpu.VMEM((width, width), bf16),
            pltpu.VMEM((width, width), bf16),
        ],
        in_specs=[SMEM] + [pl.BlockSpec(memory_space=pl.ANY)] * 6,
        out_specs=[VMEM] * 7,
        scratch_shapes=[
            pltpu.VMEM((SLOTS, rows), jnp.int32),
            pltpu.VMEM((1, rows), jnp.int32),
            pltpu.SemaphoreType.DMA((6,)),
        ],
        compiler_params=pltpu.CompilerParams(vmem_limit_bytes=24 * 2**20),
        name="slots",
    )(first_row, *stored)
    combined, sent, slopew = call(
        forward_kernel,
        [((rows, width), bf16), ((SNAPS, 2, rows // SNAPS, width), bf16), ((edges, width), bf16)],
        (from_left, own, from_right, cot, hot, weights, mproj, cproj),
        [pltpu.VMEM((3 * HALO, width), bf16)],
    )
    got = swap(sent, SNAP)
    grads, attend_part, output_part = call(
        temporal_kernel,
        [((SNAPS, rows // SNAPS, width), bf16), ((6 * width, LANES), bf16), ((2 * width, LANES), bf16)],
        (got, aproj, oproj),
        [pltpu.VMEM((2 * SNAPS * rows, 2 * width), bf16), pltpu.VMEM((2 * SNAPS * rows, width), f32)],
    )
    grad_spatial = swap(grads, SNAP).reshape(rows, width)
    to_left, to_right, own_rows, base, keep, send = call(
        backward_kernel,
        [
            ((HALO, width), bf16),
            ((HALO, width), bf16),
            ((rows, width), f32),
            ((rows, width), f32),
            ((6 * width, LANES), bf16),
            ((1, 6 * width, LANES), bf16),
        ],
        (core, grad_spatial, combined, slopew, nbrt, from_left, own, from_right, cproj, attend_part, output_part),
        [pltpu.VMEM((edges, width), bf16), pltpu.VMEM((6 * width, LANES), bf16), pltpu.VMEM((3 * HALO, edges), bf16)],
        scalars=1,
    )
    back_left = lax.ppermute(to_right, DOM, up)
    back_right = lax.ppermute(to_left, DOM, down)
    (grad_features,) = call(
        features_kernel, [((rows, width), bf16)], (base, own_rows, back_left, back_right, mproj), stored=True
    )
    both = lax.all_gather(send, "c", axis=0, tiled=True)
    count = lax.axis_size(SCATTER)
    across = lax.axis_size(ACROSS)
    piece = 6 * width // count
    (mine,) = call(pair_kernel, [((count, piece, LANES), bf16)], (core, keep, both), scalars=1)
    parts = swap(mine, SCATTER)
    (spread,) = call(fold_kernel, [((across, piece, LANES), bf16)], (parts,))
    parts = swap(spread, ACROSS)
    (whole,) = call(fold_kernel, [((count, piece, LANES), bf16)], (parts,))
    half = swap(whole, SCATTER).reshape(1, 6 * width, LANES)
    sums = lax.all_gather(half, "c", axis=0, tiled=True)
    factor = 1.0 / math.sqrt(SNAPS * dom_size * rows)

    def last(*refs):
        final_kernel(factor, *refs)

    message, combine, attend, output = call(
        last,
        [((width, width), f32), ((width, width), f32), ((width, 3 * width), f32), ((width, width), f32)],
        (sums,),
        stored=True,
    )
    return grad_features[None], message, combine, attend, output


def build(mesh, fine):
    fine_mesh = Mesh(np.asarray(mesh.devices).reshape(fine), FINE_NAMES)
    in_specs = (
        P(SNAP, DOM, None),
        P(SNAP, DOM, None),
        P(DOM, None),
        P(DOM),
        P(),
        P(),
        P(),
        P(),
    )
    out_specs = (P(SNAP, DOM, None), P(), P(), P(), P())
    return jax.shard_map(step, mesh=fine_mesh, in_specs=in_specs, out_specs=out_specs, check_vma=False)


def solution(mesh):
    return build(mesh, FINE)
```

```python
import math

import jax
import jax.numpy as jnp
import numpy as np
from jax import lax
from jax.experimental import pallas as pl
from jax.experimental.pallas import tpu as pltpu
from jax.sharding import Mesh
from jax.sharding import PartitionSpec as P


HEAD_DIM = 32
SNAPS = 8
HALO = 128
WIDTH = 256
SLOTS = 16
LANES = 128

FINE = (2, 4, 4, 2, 4, 2)
FINE_NAMES = ("zl", "x", "yh", "yl", "zh", "c")
DOM = ("zl", "x", "yh", "yl")
SNAP = ("zh", "c")
SCATTER = ("zl", "x", "yl")
ACROSS = ("yh", "zh")

f32 = jnp.float32
bf16 = jnp.bfloat16
VMEM = pl.BlockSpec(memory_space=pltpu.VMEM)
SMEM = pl.BlockSpec(memory_space=pltpu.SMEM)


def call(kernel, outs, args, scratch=(), scalars=0, stored=False):
    bound = []
    for n, a in enumerate(args):
        bound.append(a if n < scalars else pltpu.with_memory_space_constraint(a, pltpu.VMEM))
    place = jax.ShapeDtypeStruct if stored else pltpu.VMEM
    return pl.pallas_call(
        kernel,
        out_shape=[place(s, d) for s, d in outs],
        in_specs=[SMEM if n < scalars else VMEM for n in range(len(args))],
        out_specs=[VMEM] * len(outs),
        scratch_shapes=list(scratch),
        compiler_params=pltpu.CompilerParams(vmem_limit_bytes=24 * 2**20),
    )(*bound)


def mm(a, b):
    return jnp.dot(a, b, preferred_element_type=f32)


def mm_nt(a, b):
    return lax.dot_general(a, b, (((1,), (1,)), ((), ())), preferred_element_type=f32)


def mm_tn(a, b):
    return lax.dot_general(a, b, (((0,), (0,)), ((), ())), preferred_element_type=f32)


def put_slab(ref, index, value):
    base = index * 2 * WIDTH
    value = value.astype(ref.dtype)
    ref[base : base + WIDTH, :] = value[:, :LANES]
    ref[base + WIDTH : base + 2 * WIDTH, :] = value[:, LANES:]


def slots_kernel(
    first_row, nbr_in, deg_in, own, cot, mproj, cproj,
    hot, weights, nbrt, own_out, cot_out, mproj_out, cproj_out, table_in, deg, sems
):
    moves = ((nbr_in, table_in), (deg_in, deg), (own, own_out), (cot, cot_out), (mproj, mproj_out), (cproj, cproj_out))
    copies = [pltpu.make_async_copy(a, b, sems.at[n]) for n, (a, b) in enumerate(moves)]
    for copy in copies:
        copy.start()
    copies[0].wait()
    copies[1].wait()
    slots, rows = nbrt.shape
    local = table_in[...] - first_row[0]
    nbrt[...] = local
    pad = jnp.zeros((rows - slots - 1, rows), f32)
    table = jnp.concatenate([local.astype(f32), deg[...].astype(f32), pad], axis=0).T
    lanes = lax.broadcasted_iota(jnp.int32, (rows, 3 * HALO), 1).astype(f32)
    for k in range(slots):
        mark = table[:, k : k + 1] == lanes
        hot[k * rows : (k + 1) * rows] = jnp.where(mark, 1.0, 0.0).astype(bf16)
    degree = table[:, slots : slots + 1]
    slot = lax.broadcasted_iota(jnp.int32, (rows, slots), 1).astype(f32)
    weights[...] = jnp.where(slot < degree, 1.0 / degree, 0.0)
    for copy in copies[2:]:
        copy.wait()


def forward_kernel(left, own, right, cot, hot, weights, mproj, cproj, combined, sent, slopew, ext):
    ext[:HALO] = left[...]
    ext[HALO : HALO + 128] = own[...]
    ext[HALO + 128 :] = right[...]
    rows = own.shape[0]
    own_f = own[...].astype(f32)
    total = jnp.zeros((rows, WIDTH), f32)
    group = 4
    for g in range(SLOTS // group):
        span = group * rows
        picked = mm(hot[g * span : (g + 1) * span], ext[...]).astype(bf16)
        message = mm(picked, mproj[...])
        for j in range(group):
            k = g * group + j
            weight = weights[:, k : k + 1]
            before = message[j * rows : (j + 1) * rows] + own_f
            logistic = 0.5 * jnp.tanh(0.5 * before) + 0.5
            value = before * logistic
            total = total + value * weight
            slope = logistic + logistic * (before - value)
            slopew[k * rows : (k + 1) * rows] = (slope * weight).astype(bf16)
    comb = total.astype(bf16)
    combined[...] = comb
    spatial = (own_f + mm(comb, cproj[...])).astype(bf16)
    share = sent.shape[2]
    for s in range(sent.shape[0]):
        sent[s, 0] = spatial[s * share : (s + 1) * share]
        sent[s, 1] = cot[s * share : (s + 1) * share]


def temporal_kernel(got, aproj, oproj, grad_spatial, att_out, three, prods, sums):
    snaps, _, nodes, _ = got.shape
    rows = snaps * nodes
    x = got[:, 0].reshape(rows, WIDTH)
    c = got[:, 1].reshape(rows, WIDTH)
    projected = mm(x, aproj[...])
    inverse_root = 1.0 / math.sqrt(HEAD_DIM)
    qs = projected[:, :WIDTH] * inverse_root
    key = projected[:, WIDTH : 2 * WIDTH]
    val = projected[:, 2 * WIDTH :]
    da = mm_nt(c, oproj[...])

    def split(at, value):
        high = value.astype(bf16)
        prods[at : at + rows, :WIDTH] = high
        prods[at : at + rows, WIDTH:] = (value - high.astype(f32)).astype(bf16)

    key3 = key.reshape(snaps, nodes, WIDTH)
    val3 = val.reshape(snaps, nodes, WIDTH)
    for s in range(snaps):
        one = slice(s * nodes, (s + 1) * nodes)
        split(s * rows, (qs[one][None] * key3).reshape(rows, WIDTH))
        split((snaps + s) * rows, (da[one][None] * val3).reshape(rows, WIDTH))
    i = lax.broadcasted_iota(jnp.int32, (2 * WIDTH, WIDTH), 0)
    j = lax.broadcasted_iota(jnp.int32, (2 * WIDTH, WIDTH), 1)
    same = (i & (WIDTH - 1)) // HEAD_DIM == j // HEAD_DIM
    same = jnp.where(same, 1.0, 0.0).astype(bf16)
    step = 4 * rows
    for at in range(0, 2 * snaps * rows, step):
        sums[at : at + step] = mm(prods[at : at + step], same)

    grad_key = jnp.zeros((snaps, nodes, WIDTH), f32)
    grad_val = jnp.zeros((snaps, nodes, WIDTH), f32)
    attended = []
    grad_query = []
    for s in range(snaps):
        one = slice(s * nodes, (s + 1) * nodes)
        exponent = jnp.exp(sums[s * rows : (s + 1) * rows]).reshape(snaps, nodes, WIDTH)
        soft = exponent * (1.0 / jnp.sum(exponent, axis=0))[None]
        attended.append(jnp.sum(soft * val3, axis=0))
        grad_soft = sums[(snaps + s) * rows : (snaps + s + 1) * rows].reshape(snaps, nodes, WIDTH)
        mean = jnp.sum(soft * grad_soft, axis=0)
        grad_score = soft * (grad_soft - mean[None])
        grad_query.append(jnp.sum(grad_score * key3, axis=0) * inverse_root)
        grad_key = grad_key + grad_score * qs[one][None]
        grad_val = grad_val + soft * da[one][None]
    att_out[...] = jnp.concatenate(attended, axis=0).astype(bf16)
    parts = (
        jnp.concatenate(grad_query, axis=0).astype(bf16),
        grad_key.reshape(rows, WIDTH).astype(bf16),
        grad_val.reshape(rows, WIDTH).astype(bf16),
    )
    total = c.astype(f32)
    for p, part in enumerate(parts):
        three[p] = part
        total = total + mm_nt(part, aproj[:, p * WIDTH : (p + 1) * WIDTH])
    grad_spatial[...] = total.astype(bf16).reshape(snaps, nodes, WIDTH)


def halves(core, first, second, keep, send):
    mine = core[0] == 0
    for n, (a, b) in enumerate(zip(first, second)):
        a = a.astype(bf16)
        b = b.astype(bf16)
        put_slab(keep, n, jnp.where(mine, a, b))
        put_slab(send.at[0], n, jnp.where(mine, b, a))


def products_kernel(core, got, att, three, keep, send):
    snaps, _, nodes, _ = got.shape
    x = got[:, 0].reshape(snaps * nodes, WIDTH)
    c = got[:, 1].reshape(snaps * nodes, WIDTH)
    attend = [mm_tn(x, three[p]) for p in range(3)]
    halves(core, attend[:2], (attend[2], mm_tn(att[...], c)), keep, send)


def backward_kernel(
    core, gs_ref, comb, slopew, nbrt, left, own, right, cproj,
    to_left, to_right, own_rows, base, keep, send, gb, hot
):
    rows = own.shape[0]
    gs = gs_ref[...]
    gc = mm_nt(gs, cproj[...])
    total = gs.astype(f32)
    below = lax.broadcasted_iota(jnp.int32, (3 * HALO, rows), 0)
    for k in range(SLOTS):
        span = slice(k * rows, (k + 1) * rows)
        hot[:, span] = jnp.where(nbrt[k : k + 1, :] == below, 1.0, 0.0).astype(bf16)
        grad_before = gc * slopew[span].astype(f32)
        total = total + grad_before
        gb[span] = grad_before.astype(bf16)
    base[...] = total
    grad_rows = mm(hot[...], gb[...])
    rounded = grad_rows.astype(bf16)
    to_left[...] = rounded[:HALO]
    to_right[...] = rounded[HALO + rows :]
    own_rows[...] = grad_rows[HALO : HALO + rows]
    message = mm_tn(left[...], rounded[:HALO])
    message = message + mm_tn(own[...], rounded[HALO : HALO + rows])
    message = message + mm_tn(right[...], rounded[HALO + rows :])
    halves(core, (message,), (mm_tn(comb[...], gs),), keep, send)


def features_kernel(base, own_rows, from_left, from_right, mproj, grad):
    own = own_rows[...] + from_left[...].astype(f32) + from_right[...].astype(f32)
    grad[...] = (base[...] + mm_nt(own.astype(bf16), mproj[...])).astype(bf16)


def pair_kernel(core, early, early_both, late, late_both, out):
    mine = core[0] == 0

    def total(keep, both):
        other = jnp.where(mine, both[1], both[0])
        return (keep[...].astype(f32) + other.astype(f32)).astype(bf16)

    value = jnp.concatenate([total(early, early_both), total(late, late_both)], axis=0)
    out[...] = value.reshape(out.shape)


def fold_kernel(parts, out):
    total = parts[0].astype(f32)
    for p in range(1, parts.shape[0]):
        total = total + parts[p].astype(f32)
    total = total.astype(bf16)
    for p in range(out.shape[0]):
        out[p] = total


def final_kernel(factor, sums, message, combine, attend, output):
    def get(half, index):
        base = index * 2 * WIDTH
        first = sums[half, base : base + WIDTH, :].astype(f32) * factor
        second = sums[half, base + WIDTH : base + 2 * WIDTH, :].astype(f32) * factor
        return first, second

    def put(ref, at, pair):
        ref[:, at : at + LANES] = pair[0]
        ref[:, at + LANES : at + 2 * LANES] = pair[1]

    put(attend, 0, get(0, 0))
    put(attend, WIDTH, get(0, 1))
    put(attend, 2 * WIDTH, get(1, 0))
    put(output, 0, get(1, 1))
    put(message, 0, get(0, 2))
    put(combine, 0, get(1, 2))


def swap(x, axes):
    return lax.all_to_all(x, axes, split_axis=0, concat_axis=0, tiled=True)


def step(features, cotangent, neighbours, degrees, mproj, cproj, aproj, oproj):
    _, rows, width = features.shape
    dom_size = lax.axis_size(DOM)
    up = [(i, i + 1) for i in range(dom_size - 1)]
    down = [(i + 1, i) for i in range(dom_size - 1)]
    own = features[0]
    cot = cotangent[0]
    from_left = lax.ppermute(own, DOM, up)
    from_right = lax.ppermute(own, DOM, down)
    first_row = (lax.axis_index(DOM) * rows - HALO).reshape(1)
    core = lax.axis_index("c").reshape(1)
    edges = SLOTS * rows
    stored = [
        pltpu.with_memory_space_constraint(a, pltpu.HBM)
        for a in (neighbours.T, degrees.reshape(1, rows), own, cot, mproj, cproj)
    ]
    hot, weights, nbrt, own, cot, mproj, cproj = pl.pallas_call(
        slots_kernel,
        out_shape=[
            pltpu.VMEM((edges, 3 * HALO), bf16),
            pltpu.VMEM((rows, SLOTS), f32),
            pltpu.VMEM((SLOTS, rows), jnp.int32),
            pltpu.VMEM((rows, width), bf16),
            pltpu.VMEM((rows, width), bf16),
            pltpu.VMEM((width, width), bf16),
            pltpu.VMEM((width, width), bf16),
        ],
        in_specs=[SMEM] + [pl.BlockSpec(memory_space=pl.ANY)] * 6,
        out_specs=[VMEM] * 7,
        scratch_shapes=[
            pltpu.VMEM((SLOTS, rows), jnp.int32),
            pltpu.VMEM((1, rows), jnp.int32),
            pltpu.SemaphoreType.DMA((6,)),
        ],
        compiler_params=pltpu.CompilerParams(vmem_limit_bytes=24 * 2**20),
        name="slots",
    )(first_row, *stored)
    combined, sent, slopew = call(
        forward_kernel,
        [((rows, width), bf16), ((SNAPS, 2, rows // SNAPS, width), bf16), ((edges, width), bf16)],
        (from_left, own, from_right, cot, hot, weights, mproj, cproj),
        [pltpu.VMEM((3 * HALO, width), bf16)],
    )
    got = swap(sent, SNAP)
    grads, att, three = call(
        temporal_kernel,
        [((SNAPS, rows // SNAPS, width), bf16), ((rows, width), bf16), ((3, rows, width), bf16)],
        (got, aproj, oproj),
        [pltpu.VMEM((2 * SNAPS * rows, 2 * width), bf16), pltpu.VMEM((2 * SNAPS * rows, width), f32)],
    )
    grad_spatial = swap(grads, SNAP).reshape(rows, width)
    early, send = call(
        products_kernel,
        [((4 * width, LANES), bf16), ((1, 4 * width, LANES), bf16)],
        (core, got, att, three),
        scalars=1,
    )
    early_both = lax.all_gather(send, "c", axis=0, tiled=True)
    to_left, to_right, own_rows, base, keep, send = call(
        backward_kernel,
        [
            ((HALO, width), bf16),
            ((HALO, width), bf16),
            ((rows, width), f32),
            ((rows, width), f32),
            ((2 * width, LANES), bf16),
            ((1, 2 * width, LANES), bf16),
        ],
        (core, grad_spatial, combined, slopew, nbrt, from_left, own, from_right, cproj),
        [pltpu.VMEM((edges, width), bf16), pltpu.VMEM((3 * HALO, edges), bf16)],
        scalars=1,
    )
    back_left = lax.ppermute(to_right, DOM, up)
    back_right = lax.ppermute(to_left, DOM, down)
    (grad_features,) = call(
        features_kernel,
        [((rows, width), bf16)],
        (base, own_rows, back_left, back_right, mproj),
        stored=True,
    )
    late_both = lax.all_gather(send, "c", axis=0, tiled=True)
    count = lax.axis_size(SCATTER)
    across = lax.axis_size(ACROSS)
    piece = 6 * width // count
    (mine,) = call(
        pair_kernel,
        [((count, piece, LANES), bf16)],
        (core, early, early_both, keep, late_both),
        scalars=1,
    )
    parts = swap(mine, SCATTER)
    (spread,) = call(fold_kernel, [((across, piece, LANES), bf16)], (parts,))
    parts = swap(spread, ACROSS)
    (whole,) = call(fold_kernel, [((count, piece, LANES), bf16)], (parts,))
    half = swap(whole, SCATTER).reshape(1, 6 * width, LANES)
    sums = lax.all_gather(half, "c", axis=0, tiled=True)
    factor = 1.0 / math.sqrt(SNAPS * dom_size * rows)

    def last(*refs):
        final_kernel(factor, *refs)

    message, combine, attend, output = call(
        last,
        [((width, width), f32), ((width, width), f32), ((width, 3 * width), f32), ((width, width), f32)],
        (sums,),
        stored=True,
    )
    return grad_features[None], message, combine, attend, output


def build(mesh, fine):
    fine_mesh = Mesh(np.asarray(mesh.devices).reshape(fine), FINE_NAMES)
    in_specs = (
        P(SNAP, DOM, None),
        P(SNAP, DOM, None),
        P(DOM, None),
        P(DOM),
        P(),
        P(),
        P(),
        P(),
    )
    out_specs = (P(SNAP, DOM, None), P(), P(), P(), P())
    return jax.shard_map(step, mesh=fine_mesh, in_specs=in_specs, out_specs=out_specs, check_vma=False)


def solution(mesh):
    return build(mesh, FINE)
```

```python
import math

import jax
import jax.numpy as jnp
import numpy as np
from jax import lax
from jax.experimental import pallas as pl
from jax.experimental.pallas import tpu as pltpu
from jax.sharding import Mesh
from jax.sharding import PartitionSpec as P


HEAD_DIM = 32
SNAPS = 8
HALO = 128
WIDTH = 256
SLOTS = 16
LANES = 128

FINE = (2, 4, 4, 2, 4, 2)
FINE_NAMES = ("zl", "x", "yh", "yl", "zh", "c")
DOM = ("zl", "x", "yh", "yl")
SNAP = ("zh", "c")
SCATTER = ("zl", "x", "yl")
ACROSS = ("yh", "zh")

f32 = jnp.float32
bf16 = jnp.bfloat16
VMEM = pl.BlockSpec(memory_space=pltpu.VMEM)
SMEM = pl.BlockSpec(memory_space=pltpu.SMEM)


def call(kernel, outs, args, scratch=(), scalars=0, stored=False):
    bound = []
    for n, a in enumerate(args):
        bound.append(a if n < scalars else pltpu.with_memory_space_constraint(a, pltpu.VMEM))
    place = jax.ShapeDtypeStruct if stored else pltpu.VMEM
    return pl.pallas_call(
        kernel,
        out_shape=[place(s, d) for s, d in outs],
        in_specs=[SMEM if n < scalars else VMEM for n in range(len(args))],
        out_specs=[VMEM] * len(outs),
        scratch_shapes=list(scratch),
        compiler_params=pltpu.CompilerParams(vmem_limit_bytes=24 * 2**20),
    )(*bound)


def mm(a, b):
    return jnp.dot(a, b, preferred_element_type=f32)


def mm_nt(a, b):
    return lax.dot_general(a, b, (((1,), (1,)), ((), ())), preferred_element_type=f32)


def mm_tn(a, b):
    return lax.dot_general(a, b, (((0,), (0,)), ((), ())), preferred_element_type=f32)


def put_slab(ref, index, value):
    base = index * 2 * WIDTH
    value = value.astype(ref.dtype)
    ref[base : base + WIDTH, :] = value[:, :LANES]
    ref[base + WIDTH : base + 2 * WIDTH, :] = value[:, LANES:]


def slots_kernel(
    place, nbr_in, deg_in, own, cot, mproj, cproj,
    hot, weights, nbrt, own_out, cot_out, mproj_out, cproj_out, table_in, deg, sems
):
    moves = ((nbr_in, table_in), (deg_in, deg), (own, own_out), (cot, cot_out), (mproj, mproj_out), (cproj, cproj_out))
    copies = [pltpu.make_async_copy(a, b, sems.at[n]) for n, (a, b) in enumerate(moves)]
    for copy in copies:
        copy.start()
    copies[0].wait()
    copies[1].wait()
    slots, rows = nbrt.shape
    local = table_in[...] - ((place[0] >> 1) * rows - HALO)
    nbrt[...] = local
    pad = jnp.zeros((rows - slots - 1, rows), f32)
    table = jnp.concatenate([local.astype(f32), deg[...].astype(f32), pad], axis=0).T
    lanes = lax.broadcasted_iota(jnp.int32, (rows, 3 * HALO), 1).astype(f32)
    for k in range(slots):
        mark = table[:, k : k + 1] == lanes
        hot[k * rows : (k + 1) * rows] = jnp.where(mark, 1.0, 0.0).astype(bf16)
    degree = table[:, slots : slots + 1]
    slot = lax.broadcasted_iota(jnp.int32, (rows, slots), 1).astype(f32)
    weights[...] = jnp.where(slot < degree, 1.0 / degree, 0.0)
    for copy in copies[2:]:
        copy.wait()


def forward_kernel(left, own, right, cot, hot, weights, mproj, cproj, combined, sent, slopew, ext):
    ext[:HALO] = left[...]
    ext[HALO : HALO + 128] = own[...]
    ext[HALO + 128 :] = right[...]
    rows = own.shape[0]
    own_f = own[...].astype(f32)
    total = jnp.zeros((rows, WIDTH), f32)
    group = 4
    for g in range(SLOTS // group):
        span = group * rows
        picked = mm(hot[g * span : (g + 1) * span], ext[...]).astype(bf16)
        message = mm(picked, mproj[...])
        for j in range(group):
            k = g * group + j
            weight = weights[:, k : k + 1]
            before = message[j * rows : (j + 1) * rows] + own_f
            logistic = 0.5 * jnp.tanh(0.5 * before) + 0.5
            value = before * logistic
            total = total + value * weight
            slope = logistic + logistic * (before - value)
            slopew[k * rows : (k + 1) * rows] = (slope * weight).astype(bf16)
    comb = total.astype(bf16)
    combined[...] = comb
    spatial = (own_f + mm(comb, cproj[...])).astype(bf16)
    share = sent.shape[2]
    for s in range(sent.shape[0]):
        sent[s, 0] = spatial[s * share : (s + 1) * share]
        sent[s, 1] = cot[s * share : (s + 1) * share]


def temporal_kernel(got, aproj, oproj, grad_spatial, att_out, three, prods, sums):
    snaps, _, nodes, _ = got.shape
    rows = snaps * nodes
    x = got[:, 0].reshape(rows, WIDTH)
    c = got[:, 1].reshape(rows, WIDTH)
    projected = mm(x, aproj[...])
    inverse_root = 1.0 / math.sqrt(HEAD_DIM)
    qs = projected[:, :WIDTH] * inverse_root
    key = projected[:, WIDTH : 2 * WIDTH]
    val = projected[:, 2 * WIDTH :]
    da = mm_nt(c, oproj[...])

    def split(at, value):
        high = value.astype(bf16)
        prods[at : at + rows, :WIDTH] = high
        prods[at : at + rows, WIDTH:] = (value - high.astype(f32)).astype(bf16)

    key3 = key.reshape(snaps, nodes, WIDTH)
    val3 = val.reshape(snaps, nodes, WIDTH)
    for s in range(snaps):
        one = slice(s * nodes, (s + 1) * nodes)
        split(s * rows, (qs[one][None] * key3).reshape(rows, WIDTH))
        split((snaps + s) * rows, (da[one][None] * val3).reshape(rows, WIDTH))
    i = lax.broadcasted_iota(jnp.int32, (2 * WIDTH, WIDTH), 0)
    j = lax.broadcasted_iota(jnp.int32, (2 * WIDTH, WIDTH), 1)
    same = (i & (WIDTH - 1)) // HEAD_DIM == j // HEAD_DIM
    same = jnp.where(same, 1.0, 0.0).astype(bf16)
    step = 4 * rows
    for at in range(0, 2 * snaps * rows, step):
        sums[at : at + step] = mm(prods[at : at + step], same)

    grad_key = jnp.zeros((snaps, nodes, WIDTH), f32)
    grad_val = jnp.zeros((snaps, nodes, WIDTH), f32)
    attended = []
    grad_query = []
    for s in range(snaps):
        one = slice(s * nodes, (s + 1) * nodes)
        exponent = jnp.exp(sums[s * rows : (s + 1) * rows]).reshape(snaps, nodes, WIDTH)
        soft = exponent * (1.0 / jnp.sum(exponent, axis=0))[None]
        attended.append(jnp.sum(soft * val3, axis=0))
        grad_soft = sums[(snaps + s) * rows : (snaps + s + 1) * rows].reshape(snaps, nodes, WIDTH)
        mean = jnp.sum(soft * grad_soft, axis=0)
        grad_score = soft * (grad_soft - mean[None])
        grad_query.append(jnp.sum(grad_score * key3, axis=0) * inverse_root)
        grad_key = grad_key + grad_score * qs[one][None]
        grad_val = grad_val + soft * da[one][None]
    att_out[...] = jnp.concatenate(attended, axis=0).astype(bf16)
    parts = (
        jnp.concatenate(grad_query, axis=0).astype(bf16),
        grad_key.reshape(rows, WIDTH).astype(bf16),
        grad_val.reshape(rows, WIDTH).astype(bf16),
    )
    total = c.astype(f32)
    for p, part in enumerate(parts):
        three[p] = part
        total = total + mm_nt(part, aproj[:, p * WIDTH : (p + 1) * WIDTH])
    grad_spatial[...] = total.astype(bf16).reshape(snaps, nodes, WIDTH)


def halves(place, first, second, keep, send):
    mine = (place[0] & 1) == 0
    for n, (a, b) in enumerate(zip(first, second)):
        a = a.astype(bf16)
        b = b.astype(bf16)
        put_slab(keep, n, jnp.where(mine, a, b))
        put_slab(send.at[0], n, jnp.where(mine, b, a))


def products_kernel(place, got, att, three, keep, send):
    snaps, _, nodes, _ = got.shape
    x = got[:, 0].reshape(snaps * nodes, WIDTH)
    c = got[:, 1].reshape(snaps * nodes, WIDTH)
    attend = [mm_tn(x, three[p]) for p in range(3)]
    halves(place, attend[:2], (attend[2], mm_tn(att[...], c)), keep, send)


def backward_kernel(
    place, gs_ref, comb, slopew, nbrt, left, own, right, cproj,
    to_left, to_right, own_rows, base, keep, send, gb, hot
):
    rows = own.shape[0]
    gs = gs_ref[...]
    gc = mm_nt(gs, cproj[...])
    total = gs.astype(f32)
    below = lax.broadcasted_iota(jnp.int32, (3 * HALO, rows), 0)
    for k in range(SLOTS):
        span = slice(k * rows, (k + 1) * rows)
        hot[:, span] = jnp.where(nbrt[k : k + 1, :] == below, 1.0, 0.0).astype(bf16)
        grad_before = gc * slopew[span].astype(f32)
        total = total + grad_before
        gb[span] = grad_before.astype(bf16)
    base[...] = total
    grad_rows = mm(hot[...], gb[...])
    rounded = grad_rows.astype(bf16)
    to_left[...] = rounded[:HALO]
    to_right[...] = rounded[HALO + rows :]
    own_rows[...] = grad_rows[HALO : HALO + rows]
    message = mm_tn(left[...], rounded[:HALO])
    message = message + mm_tn(own[...], rounded[HALO : HALO + rows])
    message = message + mm_tn(right[...], rounded[HALO + rows :])
    halves(place, (message,), (mm_tn(comb[...], gs),), keep, send)


def features_kernel(base, own_rows, from_left, from_right, mproj, grad):
    own = own_rows[...] + from_left[...].astype(f32) + from_right[...].astype(f32)
    grad[...] = (base[...] + mm_nt(own.astype(bf16), mproj[...])).astype(bf16)


def pair_kernel(place, early, early_both, late, late_both, out):
    mine = (place[0] & 1) == 0

    def total(keep, both):
        other = jnp.where(mine, both[1], both[0])
        return (keep[...].astype(f32) + other.astype(f32)).astype(bf16)

    value = jnp.concatenate([total(early, early_both), total(late, late_both)], axis=0)
    out[...] = value.reshape(out.shape)


def fold_kernel(parts, out):
    total = parts[0].astype(f32)
    for p in range(1, parts.shape[0]):
        total = total + parts[p].astype(f32)
    total = total.astype(bf16)
    for p in range(out.shape[0]):
        out[p] = total


def final_kernel(factor, sums, message, combine, attend, output):
    def get(half, index):
        base = index * 2 * WIDTH
        first = sums[half, base : base + WIDTH, :].astype(f32) * factor
        second = sums[half, base + WIDTH : base + 2 * WIDTH, :].astype(f32) * factor
        return first, second

    def put(ref, at, pair):
        ref[:, at : at + LANES] = pair[0]
        ref[:, at + LANES : at + 2 * LANES] = pair[1]

    put(attend, 0, get(0, 0))
    put(attend, WIDTH, get(0, 1))
    put(attend, 2 * WIDTH, get(1, 0))
    put(output, 0, get(1, 1))
    put(message, 0, get(0, 2))
    put(combine, 0, get(1, 2))


def swap(x, axes):
    return lax.all_to_all(x, axes, split_axis=0, concat_axis=0, tiled=True)


def step(features, cotangent, neighbours, degrees, mproj, cproj, aproj, oproj):
    _, rows, width = features.shape
    dom_size = lax.axis_size(DOM)
    up = [(i, i + 1) for i in range(dom_size - 1)]
    down = [(i + 1, i) for i in range(dom_size - 1)]
    own = features[0]
    cot = cotangent[0]
    from_left = lax.ppermute(own, DOM, up)
    from_right = lax.ppermute(own, DOM, down)
    where = (lax.axis_index(DOM) * 2 + lax.axis_index("c")).reshape(1)
    edges = SLOTS * rows
    stored = [
        pltpu.with_memory_space_constraint(a, pltpu.HBM)
        for a in (neighbours.T, degrees.reshape(1, rows), own, cot, mproj, cproj)
    ]
    hot, weights, nbrt, own, cot, mproj, cproj = pl.pallas_call(
        slots_kernel,
        out_shape=[
            pltpu.VMEM((edges, 3 * HALO), bf16),
            pltpu.VMEM((rows, SLOTS), f32),
            pltpu.VMEM((SLOTS, rows), jnp.int32),
            pltpu.VMEM((rows, width), bf16),
            pltpu.VMEM((rows, width), bf16),
            pltpu.VMEM((width, width), bf16),
            pltpu.VMEM((width, width), bf16),
        ],
        in_specs=[SMEM] + [pl.BlockSpec(memory_space=pl.ANY)] * 6,
        out_specs=[VMEM] * 7,
        scratch_shapes=[
            pltpu.VMEM((SLOTS, rows), jnp.int32),
            pltpu.VMEM((1, rows), jnp.int32),
            pltpu.SemaphoreType.DMA((6,)),
        ],
        compiler_params=pltpu.CompilerParams(vmem_limit_bytes=24 * 2**20),
        name="slots",
    )(where, *stored)
    combined, sent, slopew = call(
        forward_kernel,
        [((rows, width), bf16), ((SNAPS, 2, rows // SNAPS, width), bf16), ((edges, width), bf16)],
        (from_left, own, from_right, cot, hot, weights, mproj, cproj),
        [pltpu.VMEM((3 * HALO, width), bf16)],
    )
    got = swap(sent, SNAP)
    grads, att, three = call(
        temporal_kernel,
        [((SNAPS, rows // SNAPS, width), bf16), ((rows, width), bf16), ((3, rows, width), bf16)],
        (got, aproj, oproj),
        [pltpu.VMEM((2 * SNAPS * rows, 2 * width), bf16), pltpu.VMEM((2 * SNAPS * rows, width), f32)],
    )
    grad_spatial = swap(grads, SNAP).reshape(rows, width)
    early, send = call(
        products_kernel,
        [((4 * width, LANES), bf16), ((1, 4 * width, LANES), bf16)],
        (where, got, att, three),
        scalars=1,
    )
    early_both = lax.all_gather(send, "c", axis=0, tiled=True)
    to_left, to_right, own_rows, base, keep, send = call(
        backward_kernel,
        [
            ((HALO, width), bf16),
            ((HALO, width), bf16),
            ((rows, width), f32),
            ((rows, width), f32),
            ((2 * width, LANES), bf16),
            ((1, 2 * width, LANES), bf16),
        ],
        (where, grad_spatial, combined, slopew, nbrt, from_left, own, from_right, cproj),
        [pltpu.VMEM((edges, width), bf16), pltpu.VMEM((3 * HALO, edges), bf16)],
        scalars=1,
    )
    back_left = lax.ppermute(to_right, DOM, up)
    back_right = lax.ppermute(to_left, DOM, down)
    (grad_features,) = call(
        features_kernel,
        [((rows, width), bf16)],
        (base, own_rows, back_left, back_right, mproj),
        stored=True,
    )
    late_both = lax.all_gather(send, "c", axis=0, tiled=True)
    count = lax.axis_size(SCATTER)
    across = lax.axis_size(ACROSS)
    piece = 6 * width // count
    (mine,) = call(
        pair_kernel,
        [((count, piece, LANES), bf16)],
        (where, early, early_both, keep, late_both),
        scalars=1,
    )
    parts = swap(mine, SCATTER)
    (spread,) = call(fold_kernel, [((across, piece, LANES), bf16)], (parts,))
    parts = swap(spread, ACROSS)
    (whole,) = call(fold_kernel, [((count, piece, LANES), bf16)], (parts,))
    half = swap(whole, SCATTER).reshape(1, 6 * width, LANES)
    sums = lax.all_gather(half, "c", axis=0, tiled=True)
    factor = 1.0 / math.sqrt(SNAPS * dom_size * rows)

    def last(*refs):
        final_kernel(factor, *refs)

    message, combine, attend, output = call(
        last,
        [((width, width), f32), ((width, width), f32), ((width, 3 * width), f32), ((width, width), f32)],
        (sums,),
        stored=True,
    )
    return grad_features[None], message, combine, attend, output


def build(mesh, fine):
    fine_mesh = Mesh(np.asarray(mesh.devices).reshape(fine), FINE_NAMES)
    in_specs = (
        P(SNAP, DOM, None),
        P(SNAP, DOM, None),
        P(DOM, None),
        P(DOM),
        P(),
        P(),
        P(),
        P(),
    )
    out_specs = (P(SNAP, DOM, None), P(), P(), P(), P())
    return jax.shard_map(step, mesh=fine_mesh, in_specs=in_specs, out_specs=out_specs, check_vma=False)


def solution(mesh):
    return build(mesh, FINE)
```

```python
import math

import jax
import jax.numpy as jnp
import numpy as np
from jax import lax
from jax.experimental import pallas as pl
from jax.experimental.pallas import tpu as pltpu
from jax.sharding import Mesh
from jax.sharding import PartitionSpec as P


HEAD_DIM = 32
SNAPS = 8
HALO = 128
WIDTH = 256
SLOTS = 16
LANES = 128

FINE = (2, 4, 4, 2, 4, 2)
FINE_NAMES = ("zl", "x", "yh", "yl", "zh", "c")
DOM = ("zl", "x", "yh", "yl")
SNAP = ("zh", "c")
SCATTER = ("zl", "x", "yl")
ACROSS = ("yh", "zh")

f32 = jnp.float32
bf16 = jnp.bfloat16
VMEM = pl.BlockSpec(memory_space=pltpu.VMEM)
SMEM = pl.BlockSpec(memory_space=pltpu.SMEM)


def call(kernel, outs, args, scratch=(), scalars=0, stored=False, own_copies=False):
    bound = []
    for n, a in enumerate(args):
        bound.append(a if n < scalars else pltpu.with_memory_space_constraint(a, pltpu.VMEM))
    place = jax.ShapeDtypeStruct if stored else pltpu.VMEM
    return pl.pallas_call(
        kernel,
        out_shape=[place(s, d) for s, d in outs],
        in_specs=[SMEM if n < scalars else VMEM for n in range(len(args))],
        out_specs=[pl.BlockSpec(memory_space=pl.ANY) if own_copies else VMEM] * len(outs),
        scratch_shapes=list(scratch),
        compiler_params=pltpu.CompilerParams(vmem_limit_bytes=24 * 2**20),
    )(*bound)


def mm(a, b):
    return jnp.dot(a, b, preferred_element_type=f32)


def mm_nt(a, b):
    return lax.dot_general(a, b, (((1,), (1,)), ((), ())), preferred_element_type=f32)


def mm_tn(a, b):
    return lax.dot_general(a, b, (((0,), (0,)), ((), ())), preferred_element_type=f32)


def put_slab(ref, index, value):
    base = index * 2 * WIDTH
    value = value.astype(ref.dtype)
    ref[base : base + WIDTH, :] = value[:, :LANES]
    ref[base + WIDTH : base + 2 * WIDTH, :] = value[:, LANES:]


def slots_kernel(
    place, nbr_in, deg_in, own, cot, mproj, cproj,
    hot, weights, nbrt, own_out, cot_out, mproj_out, cproj_out, table_in, deg, sems
):
    moves = ((nbr_in, table_in), (deg_in, deg), (own, own_out), (cot, cot_out), (mproj, mproj_out), (cproj, cproj_out))
    copies = [pltpu.make_async_copy(a, b, sems.at[n]) for n, (a, b) in enumerate(moves)]
    for copy in copies:
        copy.start()
    copies[0].wait()
    copies[1].wait()
    slots, rows = nbrt.shape
    local = table_in[...] - ((place[0] >> 1) * rows - HALO)
    nbrt[...] = local
    pad = jnp.zeros((rows - slots - 1, rows), f32)
    table = jnp.concatenate([local.astype(f32), deg[...].astype(f32), pad], axis=0).T
    lanes = lax.broadcasted_iota(jnp.int32, (rows, 3 * HALO), 1).astype(f32)
    for k in range(slots):
        mark = table[:, k : k + 1] == lanes
        hot[k * rows : (k + 1) * rows] = jnp.where(mark, 1.0, 0.0).astype(bf16)
    degree = table[:, slots : slots + 1]
    slot = lax.broadcasted_iota(jnp.int32, (rows, slots), 1).astype(f32)
    weights[...] = jnp.where(slot < degree, 0.5 / degree, 0.0)
    for copy in copies[2:]:
        copy.wait()


def forward_kernel(left, own, right, cot, hot, weights, mproj, cproj, combined, sent, slopew, ext, picked):
    ext[:HALO] = left[...]
    ext[HALO : HALO + 128] = own[...]
    ext[HALO + 128 :] = right[...]
    rows = own.shape[0]
    own_f = own[...].astype(f32)
    half_own = 0.5 * own_f
    half_proj = (0.5 * mproj[...].astype(f32)).astype(bf16)
    total = jnp.zeros((rows, WIDTH), f32)
    group = 4
    span = group * rows

    def pick(g):
        picked[g * span : (g + 1) * span] = mm(hot[g * span : (g + 1) * span], ext[...]).astype(bf16)

    pick(0)
    for g in range(SLOTS // group):
        if g + 1 < SLOTS // group:
            pick(g + 1)
        for j in range(group):
            k = g * group + j
            one = slice(k * rows, (k + 1) * rows)
            u = mm(picked[one], half_proj) + half_own
            t = jnp.tanh(u)
            share = (1.0 + t) * weights[:, k : k + 1]
            total = total + u * share
            slopew[one] = (share * (1.0 + u * (1.0 - t))).astype(bf16)
    total = total + total
    comb = total.astype(bf16)
    combined[...] = comb
    spatial = (own_f + mm(comb, cproj[...])).astype(bf16)
    share = sent.shape[2]
    for s in range(sent.shape[0]):
        sent[s, 0] = spatial[s * share : (s + 1) * share]
        sent[s, 1] = cot[s * share : (s + 1) * share]


def temporal_kernel(got, aproj, oproj, grad_spatial, att_out, three, prods, sums):
    snaps, _, nodes, _ = got.shape
    rows = snaps * nodes
    x = got[:, 0].reshape(rows, WIDTH)
    c = got[:, 1].reshape(rows, WIDTH)
    projected = mm(x, aproj[...])
    inverse_root = 1.0 / math.sqrt(HEAD_DIM)
    qs = projected[:, :WIDTH] * inverse_root
    key = projected[:, WIDTH : 2 * WIDTH]
    val = projected[:, 2 * WIDTH :]
    da = mm_nt(c, oproj[...])

    def split(at, value):
        high = value.astype(bf16)
        prods[at : at + rows, :WIDTH] = high
        prods[at : at + rows, WIDTH:] = (value - high.astype(f32)).astype(bf16)

    key3 = key.reshape(snaps, nodes, WIDTH)
    val3 = val.reshape(snaps, nodes, WIDTH)
    for s in range(snaps):
        one = slice(s * nodes, (s + 1) * nodes)
        split(s * rows, (qs[one][None] * key3).reshape(rows, WIDTH))
        split((snaps + s) * rows, (da[one][None] * val3).reshape(rows, WIDTH))
    i = lax.broadcasted_iota(jnp.int32, (2 * WIDTH, WIDTH), 0)
    j = lax.broadcasted_iota(jnp.int32, (2 * WIDTH, WIDTH), 1)
    same = (i & (WIDTH - 1)) // HEAD_DIM == j // HEAD_DIM
    same = jnp.where(same, 1.0, 0.0).astype(bf16)
    step = 4 * rows
    for at in range(0, 2 * snaps * rows, step):
        sums[at : at + step] = mm(prods[at : at + step], same)

    grad_key = jnp.zeros((snaps, nodes, WIDTH), f32)
    grad_val = jnp.zeros((snaps, nodes, WIDTH), f32)
    attended = []
    grad_query = []
    for s in range(snaps):
        one = slice(s * nodes, (s + 1) * nodes)
        exponent = jnp.exp(sums[s * rows : (s + 1) * rows]).reshape(snaps, nodes, WIDTH)
        soft = exponent * (1.0 / jnp.sum(exponent, axis=0))[None]
        attended.append(jnp.sum(soft * val3, axis=0))
        grad_soft = sums[(snaps + s) * rows : (snaps + s + 1) * rows].reshape(snaps, nodes, WIDTH)
        mean = jnp.sum(soft * grad_soft, axis=0)
        grad_score = soft * (grad_soft - mean[None])
        grad_query.append(jnp.sum(grad_score * key3, axis=0) * inverse_root)
        grad_key = grad_key + grad_score * qs[one][None]
        grad_val = grad_val + soft * da[one][None]
    att_out[...] = jnp.concatenate(attended, axis=0).astype(bf16)
    parts = (
        jnp.concatenate(grad_query, axis=0).astype(bf16),
        grad_key.reshape(rows, WIDTH).astype(bf16),
        grad_val.reshape(rows, WIDTH).astype(bf16),
    )
    total = c.astype(f32)
    for p, part in enumerate(parts):
        three[p] = part
        total = total + mm_nt(part, aproj[:, p * WIDTH : (p + 1) * WIDTH])
    grad_spatial[...] = total.astype(bf16).reshape(snaps, nodes, WIDTH)


def halves(place, first, second, keep, send):
    mine = (place[0] & 1) == 0
    for n, (a, b) in enumerate(zip(first, second)):
        a = a.astype(bf16)
        b = b.astype(bf16)
        put_slab(keep, n, jnp.where(mine, a, b))
        put_slab(send.at[0], n, jnp.where(mine, b, a))


def products_kernel(place, got, att, three, keep, send):
    snaps, _, nodes, _ = got.shape
    x = got[:, 0].reshape(snaps * nodes, WIDTH)
    c = got[:, 1].reshape(snaps * nodes, WIDTH)
    attend = [mm_tn(x, three[p]) for p in range(3)]
    halves(place, attend[:2], (attend[2], mm_tn(att[...], c)), keep, send)


def backward_kernel(
    place, gs_ref, comb, slopew, nbrt, left, own, right, cproj,
    to_left, to_right, own_rows, base, keep, send, gb, hot
):
    rows = own.shape[0]
    gs = gs_ref[...]
    gc = mm_nt(gs, cproj[...])
    total = gs.astype(f32)
    below = lax.broadcasted_iota(jnp.int32, (HALO, rows), 0).astype(f32).astype(bf16)
    one = jnp.ones((HALO, rows), bf16)
    nbr = nbrt[...]
    for part in range(3):
        near = nbr - part * HALO
        near = jnp.where((near >= 0) & (near < HALO), near, -1).astype(f32).astype(bf16)
        for k in range(SLOTS):
            mark = near[k : k + 1, :] == below
            hot[part * HALO : (part + 1) * HALO, k * rows : (k + 1) * rows] = jnp.where(mark, one, 0 * one)
    for k in range(SLOTS):
        span = slice(k * rows, (k + 1) * rows)
        grad_before = gc * slopew[span].astype(f32)
        total = total + grad_before
        gb[span] = grad_before.astype(bf16)
    base[...] = total
    grad_rows = mm(hot[...], gb[...])
    rounded = grad_rows.astype(bf16)
    to_left[...] = rounded[:HALO]
    to_right[...] = rounded[HALO + rows :]
    own_rows[...] = grad_rows[HALO : HALO + rows]
    message = mm_tn(left[...], rounded[:HALO])
    message = message + mm_tn(own[...], rounded[HALO : HALO + rows])
    message = message + mm_tn(right[...], rounded[HALO + rows :])
    halves(place, (message,), (mm_tn(comb[...], gs),), keep, send)


def features_kernel(base, own_rows, from_left, from_right, mproj, grad):
    own = own_rows[...] + from_left[...].astype(f32) + from_right[...].astype(f32)
    grad[...] = (base[...] + mm_nt(own.astype(bf16), mproj[...])).astype(bf16)


def pair_kernel(place, early, early_both, late, late_both, out):
    mine = (place[0] & 1) == 0

    def total(keep, both):
        other = jnp.where(mine, both[1], both[0])
        return (keep[...].astype(f32) + other.astype(f32)).astype(bf16)

    value = jnp.concatenate([total(early, early_both), total(late, late_both)], axis=0)
    out[...] = value.reshape(out.shape)


def fold_kernel(parts, out):
    total = parts[0].astype(f32)
    for p in range(1, parts.shape[0]):
        total = total + parts[p].astype(f32)
    total = total.astype(bf16)
    for p in range(out.shape[0]):
        out[p] = total


def spread_kernel(parts, out, total_ref, sems):
    total = parts[0].astype(f32)
    for p in range(1, parts.shape[0]):
        total = total + parts[p].astype(f32)
    total_ref[...] = total.astype(bf16)
    copies = [pltpu.make_async_copy(total_ref, out.at[p], sems.at[p]) for p in range(out.shape[0])]
    for copy in copies:
        copy.start()
    for copy in copies:
        copy.wait()


def final_kernel(factor, sums, message, combine, attend, output, blocks, sems):
    places = (
        (attend.at[:, :WIDTH], 0, 0),
        (attend.at[:, WIDTH : 2 * WIDTH], 0, 1),
        (attend.at[:, 2 * WIDTH :], 1, 0),
        (output, 1, 1),
        (message, 0, 2),
        (combine, 1, 2),
    )
    copies = []
    for n, (target, half, index) in enumerate(places):
        base = index * 2 * WIDTH
        blocks[n, :, :LANES] = sums[half, base : base + WIDTH, :].astype(f32) * factor
        blocks[n, :, LANES:] = sums[half, base + WIDTH : base + 2 * WIDTH, :].astype(f32) * factor
        copies.append(pltpu.make_async_copy(blocks.at[n], target, sems.at[n]))
        copies[-1].start()
    for copy in copies:
        copy.wait()


def swap(x, axes):
    return lax.all_to_all(x, axes, split_axis=0, concat_axis=0, tiled=True)


def step(features, cotangent, neighbours, degrees, mproj, cproj, aproj, oproj):
    _, rows, width = features.shape
    dom_size = lax.axis_size(DOM)
    up = [(i, i + 1) for i in range(dom_size - 1)]
    down = [(i + 1, i) for i in range(dom_size - 1)]
    own = features[0]
    cot = cotangent[0]
    from_left = lax.ppermute(own, DOM, up)
    from_right = lax.ppermute(own, DOM, down)
    where = (lax.axis_index(DOM) * 2 + lax.axis_index("c")).reshape(1)
    edges = SLOTS * rows
    stored = [
        pltpu.with_memory_space_constraint(a, pltpu.HBM)
        for a in (neighbours.T, degrees.reshape(1, rows), own, cot, mproj, cproj)
    ]
    hot, weights, nbrt, own, cot, mproj, cproj = pl.pallas_call(
        slots_kernel,
        out_shape=[
            pltpu.VMEM((edges, 3 * HALO), bf16),
            pltpu.VMEM((rows, SLOTS), f32),
            pltpu.VMEM((SLOTS, rows), jnp.int32),
            pltpu.VMEM((rows, width), bf16),
            pltpu.VMEM((rows, width), bf16),
            pltpu.VMEM((width, width), bf16),
            pltpu.VMEM((width, width), bf16),
        ],
        in_specs=[SMEM] + [pl.BlockSpec(memory_space=pl.ANY)] * 6,
        out_specs=[VMEM] * 7,
        scratch_shapes=[
            pltpu.VMEM((SLOTS, rows), jnp.int32),
            pltpu.VMEM((1, rows), jnp.int32),
            pltpu.SemaphoreType.DMA((6,)),
        ],
        compiler_params=pltpu.CompilerParams(vmem_limit_bytes=24 * 2**20),
        name="slots",
    )(where, *stored)
    combined, sent, slopew = call(
        forward_kernel,
        [((rows, width), bf16), ((SNAPS, 2, rows // SNAPS, width), bf16), ((edges, width), bf16)],
        (from_left, own, from_right, cot, hot, weights, mproj, cproj),
        [
            pltpu.VMEM((3 * HALO, width), bf16),
            pltpu.VMEM((edges, width), bf16),
        ],
    )
    got = swap(sent, SNAP)
    grads, att, three = call(
        temporal_kernel,
        [((SNAPS, rows // SNAPS, width), bf16), ((rows, width), bf16), ((3, rows, width), bf16)],
        (got, aproj, oproj),
        [pltpu.VMEM((2 * SNAPS * rows, 2 * width), bf16), pltpu.VMEM((2 * SNAPS * rows, width), f32)],
    )
    grad_spatial = swap(grads, SNAP).reshape(rows, width)
    early, send = call(
        products_kernel,
        [((4 * width, LANES), bf16), ((1, 4 * width, LANES), bf16)],
        (where, got, att, three),
        scalars=1,
    )
    early_both = lax.all_gather(send, "c", axis=0, tiled=True)
    to_left, to_right, own_rows, base, keep, send = call(
        backward_kernel,
        [
            ((HALO, width), bf16),
            ((HALO, width), bf16),
            ((rows, width), f32),
            ((rows, width), f32),
            ((2 * width, LANES), bf16),
            ((1, 2 * width, LANES), bf16),
        ],
        (where, grad_spatial, combined, slopew, nbrt, from_left, own, from_right, cproj),
        [pltpu.VMEM((edges, width), bf16), pltpu.VMEM((3 * HALO, edges), bf16)],
        scalars=1,
    )
    back_left = lax.ppermute(to_right, DOM, up)
    back_right = lax.ppermute(to_left, DOM, down)
    (grad_features,) = call(
        features_kernel, [((rows, width), bf16)], (base, own_rows, back_left, back_right, mproj), stored=True
    )
    late_both = lax.all_gather(send, "c", axis=0, tiled=True)
    count = lax.axis_size(SCATTER)
    across = lax.axis_size(ACROSS)
    piece = 6 * width // count
    (mine,) = call(pair_kernel, [((count, piece, LANES), bf16)], (where, early, early_both, keep, late_both), scalars=1)
    parts = swap(mine, SCATTER)
    (spread,) = call(
        spread_kernel,
        [((across, piece, LANES), bf16)],
        (parts,),
        [pltpu.VMEM((piece, LANES), bf16), pltpu.SemaphoreType.DMA((across,))],
        stored=True,
        own_copies=True,
    )
    parts = swap(spread, ACROSS)
    (whole,) = call(fold_kernel, [((count, piece, LANES), bf16)], (parts,))
    half = swap(whole, SCATTER).reshape(1, 6 * width, LANES)
    sums = lax.all_gather(half, "c", axis=0, tiled=True)
    factor = 1.0 / math.sqrt(SNAPS * dom_size * rows)

    def last(*refs):
        final_kernel(factor, *refs)

    message, combine, attend, output = call(
        last,
        [((width, width), f32), ((width, width), f32), ((width, 3 * width), f32), ((width, width), f32)],
        (sums,),
        [pltpu.VMEM((6, width, width), f32), pltpu.SemaphoreType.DMA((6,))],
        stored=True,
        own_copies=True,
    )
    return grad_features[None], message, combine, attend, output


def build(mesh, fine):
    fine_mesh = Mesh(np.asarray(mesh.devices).reshape(fine), FINE_NAMES)
    in_specs = (
        P(SNAP, DOM, None),
        P(SNAP, DOM, None),
        P(DOM, None),
        P(DOM),
        P(),
        P(),
        P(),
        P(),
    )
    out_specs = (P(SNAP, DOM, None), P(), P(), P(), P())
    return jax.shard_map(step, mesh=fine_mesh, in_specs=in_specs, out_specs=out_specs, check_vma=False)


def solution(mesh):
    return build(mesh, FINE)
```

```python
import math

import jax
import jax.numpy as jnp
import numpy as np
from jax import lax
from jax.experimental import pallas as pl
from jax.experimental.pallas import tpu as pltpu
from jax.sharding import Mesh
from jax.sharding import PartitionSpec as P


HEAD_DIM = 32
SNAPS = 8
HALO = 128
WIDTH = 256
SLOTS = 16
LANES = 128

FINE = (2, 4, 4, 2, 4, 2)
FINE_NAMES = ("zl", "x", "yh", "yl", "zh", "c")
DOM = ("zl", "x", "yh", "yl")
SNAP = ("zh", "c")
SCATTER = ("x", "zl", "yl")
ACROSS = ("yh", "zh")

f32 = jnp.float32
bf16 = jnp.bfloat16
VMEM = pl.BlockSpec(memory_space=pltpu.VMEM)
SMEM = pl.BlockSpec(memory_space=pltpu.SMEM)


def call(kernel, outs, args, scratch=(), scalars=0, stored=False, own_copies=False):
    bound = []
    for n, a in enumerate(args):
        bound.append(a if n < scalars else pltpu.with_memory_space_constraint(a, pltpu.VMEM))
    place = jax.ShapeDtypeStruct if stored else pltpu.VMEM
    return pl.pallas_call(
        kernel,
        out_shape=[place(s, d) for s, d in outs],
        in_specs=[SMEM if n < scalars else VMEM for n in range(len(args))],
        out_specs=[pl.BlockSpec(memory_space=pl.ANY) if own_copies else VMEM] * len(outs),
        scratch_shapes=list(scratch),
        compiler_params=pltpu.CompilerParams(vmem_limit_bytes=24 * 2**20),
    )(*bound)


def mm(a, b):
    return jnp.dot(a, b, preferred_element_type=f32)


def mm_nt(a, b):
    return lax.dot_general(a, b, (((1,), (1,)), ((), ())), preferred_element_type=f32)


def mm_tn(a, b):
    return lax.dot_general(a, b, (((0,), (0,)), ((), ())), preferred_element_type=f32)


def put_slab(ref, index, value):
    base = index * 2 * WIDTH
    value = value.astype(ref.dtype)
    ref[base : base + WIDTH, :] = value[:, :LANES]
    ref[base + WIDTH : base + 2 * WIDTH, :] = value[:, LANES:]


def slots_kernel(
    place, nbr_in, deg_in, own, cot, mproj, cproj,
    hot, weights, nbrt, own_out, cot_out, mproj_out, cproj_out, table_in, deg, sems
):
    moves = ((nbr_in, table_in), (deg_in, deg), (own, own_out), (cot, cot_out), (mproj, mproj_out), (cproj, cproj_out))
    copies = [pltpu.make_async_copy(a, b, sems.at[n]) for n, (a, b) in enumerate(moves)]
    for copy in copies:
        copy.start()
    copies[0].wait()
    copies[1].wait()
    slots, rows = nbrt.shape
    local = table_in[...] - ((place[0] >> 1) * rows - HALO)
    nbrt[...] = local
    pad = jnp.zeros((rows - slots - 1, rows), f32)
    table = jnp.concatenate([local.astype(f32), deg[...].astype(f32), pad], axis=0).T
    lanes = lax.broadcasted_iota(jnp.int32, (rows, 3 * HALO), 1).astype(f32)
    for k in range(slots):
        mark = table[:, k : k + 1] == lanes
        hot[k * rows : (k + 1) * rows] = jnp.where(mark, 1.0, 0.0).astype(bf16)
    degree = table[:, slots : slots + 1]
    slot = lax.broadcasted_iota(jnp.int32, (rows, slots), 1).astype(f32)
    weights[...] = jnp.where(slot < degree, 0.5 / degree, 0.0)
    for copy in copies[2:]:
        copy.wait()


def forward_kernel(left, own, right, cot, hot, weights, mproj, cproj, combined, sent, slopew, ext, picked):
    ext[:HALO] = left[...]
    ext[HALO : HALO + 128] = own[...]
    ext[HALO + 128 :] = right[...]
    rows = own.shape[0]
    own_f = own[...].astype(f32)
    half_own = 0.5 * own_f
    half_proj = (0.5 * mproj[...].astype(f32)).astype(bf16)
    total = jnp.zeros((rows, WIDTH), f32)
    group = 4
    span = group * rows

    def pick(g):
        picked[g * span : (g + 1) * span] = mm(hot[g * span : (g + 1) * span], ext[...]).astype(bf16)

    pick(0)
    for g in range(SLOTS // group):
        if g + 1 < SLOTS // group:
            pick(g + 1)
        for j in range(group):
            k = g * group + j
            one = slice(k * rows, (k + 1) * rows)
            u = mm(picked[one], half_proj) + half_own
            t = jnp.tanh(u)
            share = (1.0 + t) * weights[:, k : k + 1]
            total = total + u * share
            slopew[one] = (share * (1.0 + u * (1.0 - t))).astype(bf16)
    total = total + total
    comb = total.astype(bf16)
    combined[...] = comb
    spatial = (own_f + mm(comb, cproj[...])).astype(bf16)
    share = sent.shape[2]
    for s in range(sent.shape[0]):
        sent[s, 0] = spatial[s * share : (s + 1) * share]
        sent[s, 1] = cot[s * share : (s + 1) * share]


def temporal_kernel(got, aproj, oproj, grad_spatial, att_out, three, prods, sums):
    snaps, _, nodes, _ = got.shape
    rows = snaps * nodes
    x = got[:, 0].reshape(rows, WIDTH)
    c = got[:, 1].reshape(rows, WIDTH)
    projected = mm(x, aproj[...])
    inverse_root = 1.0 / math.sqrt(HEAD_DIM)
    qs = projected[:, :WIDTH] * inverse_root
    key = projected[:, WIDTH : 2 * WIDTH]
    val = projected[:, 2 * WIDTH :]
    da = mm_nt(c, oproj[...])

    def split(at, value):
        high = value.astype(bf16)
        prods[at : at + rows, :WIDTH] = high
        prods[at : at + rows, WIDTH:] = (value - high.astype(f32)).astype(bf16)

    key3 = key.reshape(snaps, nodes, WIDTH)
    val3 = val.reshape(snaps, nodes, WIDTH)
    for s in range(snaps):
        one = slice(s * nodes, (s + 1) * nodes)
        split(s * rows, (qs[one][None] * key3).reshape(rows, WIDTH))
        split((snaps + s) * rows, (da[one][None] * val3).reshape(rows, WIDTH))
    i = lax.broadcasted_iota(jnp.int32, (2 * WIDTH, WIDTH), 0)
    j = lax.broadcasted_iota(jnp.int32, (2 * WIDTH, WIDTH), 1)
    same = (i & (WIDTH - 1)) // HEAD_DIM == j // HEAD_DIM
    same = jnp.where(same, 1.0, 0.0).astype(bf16)
    step = 4 * rows
    for at in range(0, 2 * snaps * rows, step):
        sums[at : at + step] = mm(prods[at : at + step], same)

    grad_key = jnp.zeros((snaps, nodes, WIDTH), f32)
    grad_val = jnp.zeros((snaps, nodes, WIDTH), f32)
    attended = []
    grad_query = []
    for s in range(snaps):
        one = slice(s * nodes, (s + 1) * nodes)
        exponent = jnp.exp(sums[s * rows : (s + 1) * rows]).reshape(snaps, nodes, WIDTH)
        soft = exponent * (1.0 / jnp.sum(exponent, axis=0))[None]
        attended.append(jnp.sum(soft * val3, axis=0))
        grad_soft = sums[(snaps + s) * rows : (snaps + s + 1) * rows].reshape(snaps, nodes, WIDTH)
        mean = jnp.sum(soft * grad_soft, axis=0)
        grad_score = soft * (grad_soft - mean[None])
        grad_query.append(jnp.sum(grad_score * key3, axis=0) * inverse_root)
        grad_key = grad_key + grad_score * qs[one][None]
        grad_val = grad_val + soft * da[one][None]
    att_out[...] = jnp.concatenate(attended, axis=0).astype(bf16)
    parts = (
        jnp.concatenate(grad_query, axis=0).astype(bf16),
        grad_key.reshape(rows, WIDTH).astype(bf16),
        grad_val.reshape(rows, WIDTH).astype(bf16),
    )
    total = c.astype(f32)
    for p, part in enumerate(parts):
        three[p] = part
        total = total + mm_nt(part, aproj[:, p * WIDTH : (p + 1) * WIDTH])
    grad_spatial[...] = total.astype(bf16).reshape(snaps, nodes, WIDTH)


def halves(place, first, second, keep, send):
    mine = (place[0] & 1) == 0
    for n, (a, b) in enumerate(zip(first, second)):
        a = a.astype(bf16)
        b = b.astype(bf16)
        put_slab(keep, n, jnp.where(mine, a, b))
        put_slab(send.at[0], n, jnp.where(mine, b, a))


def products_kernel(place, got, att, three, keep, send):
    snaps, _, nodes, _ = got.shape
    x = got[:, 0].reshape(snaps * nodes, WIDTH)
    c = got[:, 1].reshape(snaps * nodes, WIDTH)
    attend = [mm_tn(x, three[p]) for p in range(3)]
    halves(place, attend[:2], (attend[2], mm_tn(att[...], c)), keep, send)


def backward_kernel(
    place, gs_ref, comb, slopew, nbrt, left, own, right, cproj,
    to_left, to_right, own_rows, base, keep, send, gb, hot
):
    rows = own.shape[0]
    gs = gs_ref[...]
    gc = mm_nt(gs, cproj[...])
    total = gs.astype(f32)
    below = lax.broadcasted_iota(jnp.int32, (HALO, rows), 0).astype(f32).astype(bf16)
    one = jnp.ones((HALO, rows), bf16)
    nbr = nbrt[...]
    for part in range(3):
        near = nbr - part * HALO
        near = jnp.where((near >= 0) & (near < HALO), near, -1).astype(f32).astype(bf16)
        for k in range(SLOTS):
            mark = near[k : k + 1, :] == below
            hot[part * HALO : (part + 1) * HALO, k * rows : (k + 1) * rows] = jnp.where(mark, one, 0 * one)
    for k in range(SLOTS):
        span = slice(k * rows, (k + 1) * rows)
        grad_before = gc * slopew[span].astype(f32)
        total = total + grad_before
        gb[span] = grad_before.astype(bf16)
    base[...] = total
    grad_rows = mm(hot[...], gb[...])
    rounded = grad_rows.astype(bf16)
    to_left[...] = rounded[:HALO]
    to_right[...] = rounded[HALO + rows :]
    own_rows[...] = grad_rows[HALO : HALO + rows]
    message = mm_tn(left[...], rounded[:HALO])
    message = message + mm_tn(own[...], rounded[HALO : HALO + rows])
    message = message + mm_tn(right[...], rounded[HALO + rows :])
    halves(place, (message,), (mm_tn(comb[...], gs),), keep, send)


def features_kernel(base, own_rows, from_left, from_right, mproj, grad):
    own = own_rows[...] + from_left[...].astype(f32) + from_right[...].astype(f32)
    grad[...] = (base[...] + mm_nt(own.astype(bf16), mproj[...])).astype(bf16)


def pair_kernel(place, early, early_both, late, late_both, out):
    mine = (place[0] & 1) == 0

    def total(keep, both):
        other = jnp.where(mine, both[1], both[0])
        return (keep[...].astype(f32) + other.astype(f32)).astype(bf16)

    value = jnp.concatenate([total(early, early_both), total(late, late_both)], axis=0)
    out[...] = value.reshape(out.shape)


def fold_kernel(parts, out):
    total = parts[0].astype(f32)
    for p in range(1, parts.shape[0]):
        total = total + parts[p].astype(f32)
    total = total.astype(bf16)
    for p in range(out.shape[0]):
        out[p] = total


def final_kernel(factor, sums, message, combine, attend, output, blocks, sems):
    places = (
        (attend.at[:, :WIDTH], 0, 0),
        (attend.at[:, WIDTH : 2 * WIDTH], 0, 1),
        (attend.at[:, 2 * WIDTH :], 1, 0),
        (output, 1, 1),
        (message, 0, 2),
        (combine, 1, 2),
    )
    copies = []
    for n, (target, half, index) in enumerate(places):
        base = index * 2 * WIDTH
        blocks[n, :, :LANES] = sums[half, base : base + WIDTH, :].astype(f32) * factor
        blocks[n, :, LANES:] = sums[half, base + WIDTH : base + 2 * WIDTH, :].astype(f32) * factor
        copies.append(pltpu.make_async_copy(blocks.at[n], target, sems.at[n]))
        copies[-1].start()
    for copy in copies:
        copy.wait()


def swap(x, axes):
    return lax.all_to_all(x, axes, split_axis=0, concat_axis=0, tiled=True)


def step(features, cotangent, neighbours, degrees, mproj, cproj, aproj, oproj):
    _, rows, width = features.shape
    dom_size = lax.axis_size(DOM)
    up = [(i, i + 1) for i in range(dom_size - 1)]
    down = [(i + 1, i) for i in range(dom_size - 1)]
    own = features[0]
    cot = cotangent[0]
    from_left = lax.ppermute(own, DOM, up)
    from_right = lax.ppermute(own, DOM, down)
    where = (lax.axis_index(DOM) * 2 + lax.axis_index("c")).reshape(1)
    edges = SLOTS * rows
    stored = [
        pltpu.with_memory_space_constraint(a, pltpu.HBM)
        for a in (neighbours.T, degrees.reshape(1, rows), own, cot, mproj, cproj)
    ]
    hot, weights, nbrt, own, cot, mproj, cproj = pl.pallas_call(
        slots_kernel,
        out_shape=[
            pltpu.VMEM((edges, 3 * HALO), bf16),
            pltpu.VMEM((rows, SLOTS), f32),
            pltpu.VMEM((SLOTS, rows), jnp.int32),
            pltpu.VMEM((rows, width), bf16),
            pltpu.VMEM((rows, width), bf16),
            pltpu.VMEM((width, width), bf16),
            pltpu.VMEM((width, width), bf16),
        ],
        in_specs=[SMEM] + [pl.BlockSpec(memory_space=pl.ANY)] * 6,
        out_specs=[VMEM] * 7,
        scratch_shapes=[
            pltpu.VMEM((SLOTS, rows), jnp.int32),
            pltpu.VMEM((1, rows), jnp.int32),
            pltpu.SemaphoreType.DMA((6,)),
        ],
        compiler_params=pltpu.CompilerParams(vmem_limit_bytes=24 * 2**20),
        name="slots",
    )(where, *stored)
    combined, sent, slopew = call(
        forward_kernel,
        [((rows, width), bf16), ((SNAPS, 2, rows // SNAPS, width), bf16), ((edges, width), bf16)],
        (from_left, own, from_right, cot, hot, weights, mproj, cproj),
        [
            pltpu.VMEM((3 * HALO, width), bf16),
            pltpu.VMEM((edges, width), bf16),
        ],
    )
    got = swap(sent, SNAP)
    grads, att, three = call(
        temporal_kernel,
        [((SNAPS, rows // SNAPS, width), bf16), ((rows, width), bf16), ((3, rows, width), bf16)],
        (got, aproj, oproj),
        [pltpu.VMEM((2 * SNAPS * rows, 2 * width), bf16), pltpu.VMEM((2 * SNAPS * rows, width), f32)],
    )
    grad_spatial = swap(grads, SNAP).reshape(rows, width)
    early, send = call(
        products_kernel,
        [((4 * width, LANES), bf16), ((1, 4 * width, LANES), bf16)],
        (where, got, att, three),
        scalars=1,
    )
    early_both = lax.all_gather(send, "c", axis=0, tiled=True)
    to_left, to_right, own_rows, base, keep, send = call(
        backward_kernel,
        [
            ((HALO, width), bf16),
            ((HALO, width), bf16),
            ((rows, width), f32),
            ((rows, width), f32),
            ((2 * width, LANES), bf16),
            ((1, 2 * width, LANES), bf16),
        ],
        (where, grad_spatial, combined, slopew, nbrt, from_left, own, from_right, cproj),
        [pltpu.VMEM((edges, width), bf16), pltpu.VMEM((3 * HALO, edges), bf16)],
        scalars=1,
    )
    back_left = lax.ppermute(to_right, DOM, up)
    back_right = lax.ppermute(to_left, DOM, down)
    (grad_features,) = call(
        features_kernel, [((rows, width), bf16)], (base, own_rows, back_left, back_right, mproj), stored=True
    )
    late_both = lax.all_gather(send, "c", axis=0, tiled=True)
    count = lax.axis_size(SCATTER)
    across = lax.axis_size(ACROSS)
    piece = 6 * width // count
    (mine,) = call(pair_kernel, [((count, piece, LANES), bf16)], (where, early, early_both, keep, late_both), scalars=1)
    parts = swap(mine, SCATTER)
    (spread,) = call(fold_kernel, [((across, piece, LANES), bf16)], (parts,))
    parts = swap(spread, ACROSS)
    (whole,) = call(fold_kernel, [((count, piece, LANES), bf16)], (parts,))
    half = swap(whole, SCATTER).reshape(1, 6 * width, LANES)
    sums = lax.all_gather(half, "c", axis=0, tiled=True)
    factor = 1.0 / math.sqrt(SNAPS * dom_size * rows)

    def last(*refs):
        final_kernel(factor, *refs)

    message, combine, attend, output = call(
        last,
        [((width, width), f32), ((width, width), f32), ((width, 3 * width), f32), ((width, width), f32)],
        (sums,),
        [pltpu.VMEM((6, width, width), f32), pltpu.SemaphoreType.DMA((6,))],
        stored=True,
        own_copies=True,
    )
    return grad_features[None], message, combine, attend, output


def build(mesh, fine):
    fine_mesh = Mesh(np.asarray(mesh.devices).reshape(fine), FINE_NAMES)
    in_specs = (
        P(SNAP, DOM, None),
        P(SNAP, DOM, None),
        P(DOM, None),
        P(DOM),
        P(),
        P(),
        P(),
        P(),
    )
    out_specs = (P(SNAP, DOM, None), P(), P(), P(), P())
    return jax.shard_map(step, mesh=fine_mesh, in_specs=in_specs, out_specs=out_specs, check_vma=False)


def solution(mesh):
    return build(mesh, FINE)
```
